128 devices in a mesh: list: 8 (over z, core), fsdp: 16 (over x, y).
Axes of the slice: x: 4, y: 4, z: 4, core: 2. Of those that a mesh axis runs over, the one named last changes fastest.
Arguments:
- hidden: bfloat16 [2048, 64, 2048], P(('list', 'fsdp')), may hold values from -6 to 6
- norm_gain: float32 [2048], replicated, may hold values from 0.5 to 1.5
- w_qkv: bfloat16 [2048, 1536], P('fsdp'), may hold values from -0.125 to 0.125
- w_out: bfloat16 [1024, 2048], P('fsdp'), may hold values from -0.1875 to 0.1875
- final_gain: float32 [2048], replicated, may hold values from 0.5 to 1.5
- w_score: float32 [2048], replicated, may hold values from -0.125 to 0.125
- prior: float32 [2048], P(('list', 'fsdp')), may hold values from -8 to 400
- labels: int32 [2048], P(('list', 'fsdp')), may hold values from 0 to 3
- lengths: int32 [64], replicated, may hold values from 1 to 48, 2048 in all
Outputs:
- loss: float32 [], replicated
- grad_qkv: float32 [2048, 1536], P('fsdp', 'list')
- grad_out: float32 [1024, 2048], P('fsdp', 'list')
The draws below stay inside these ranges and needn't reach their ends.
Inputs may be any that keep to these rules, and one draw needn't show every extreme that they name: `lengths`: the longest list holds exactly 48 passages.
All inputs are finite; a program needn't handle non-finite values.
Results may differ from the reference program's by a relative error of at most 0.025.
Values may be sent and summed in bfloat16 or wider, within the bound.
A program may use at most 128 MiB of HBM per device.

```python
import math
import jax
import jax.numpy as jnp
import numpy as np
from jax import lax

D = 2048
HEADS = 16
KV_HEADS = 4
HEAD_DIM = 64
PASSAGE_LEN = 64
LONGEST = 48
PASSAGES_DEV = 16
PASSAGES = 2048
QUERIES = 64
N_LIST = 8
N_FSDP = 16


def draw_prior(key, part):
    second_key = jax.random.fold_in(jax.random.fold_in(key, 17), 1)
    return jnp.clip(jax.random.normal(second_key, (PASSAGES,), jnp.float32), -6.0, 6.0)


def plant(result, rng, low, high):
    spot = [jax.random.randint(jax.random.fold_in(rng, axis), (), 0, length) for axis, length in enumerate(result.shape)]
    longest = result.shape.index(max(result.shape))
    next_to = spot[:longest] + [(spot[longest] + 1) % result.shape[longest]] + spot[longest + 1:]
    return result.at[tuple(spot)].set(low).at[tuple(next_to)].set(high)


def block_scale(rng, extent, cuts, least, top_value):
    factor_of = 1.0
    for axis_at, shards_of in cuts:
        steps = jax.random.uniform(jax.random.fold_in(jax.random.fold_in(rng, 6), axis_at), (shards_of,), jnp.float32, least / len(cuts), top_value / len(cuts))
        factor_of = factor_of * jnp.repeat(jnp.exp(steps), extent[axis_at] // shards_of).reshape((-1,) + (1,) * (len(extent) - 1 - axis_at))
    return factor_of


def profile(number_of, total, reach, skew):
    portions = [(1 << 20) // math.isqrt(standing ** skew) + 1 for standing in range(2, number_of + 1)]
    spare, given = total - reach - (number_of - 1), [1] * (number_of - 1)
    while spare > 0:
        free = [i for i in range(number_of - 1) if given[i] < reach]
        pool, left = sum([portions[i] for i in free]), spare
        for i in free:
            addition = min(reach - given[i], max(1, left * portions[i] // pool), spare)
            given[i] = given[i] + addition
            spare = spare - addition
    return np.array([reach] + given)


def uneven(rng, amount, total, bound, slope):
    if amount == 2:
        one = jax.random.randint(rng, (), max(1, total - bound), min(bound, total - 1) + 1)
        return jnp.stack([one, total - one])
    sizes = jnp.asarray(profile(amount, total, bound, slope), jnp.int32)
    twos = (amount - 1) // 2
    donor, taker = sizes[1:1 + 2 * twos:2], sizes[2:2 + 2 * twos:2]
    slack = jnp.minimum(donor - 1, bound - taker)
    moved = jax.random.randint(jax.random.fold_in(rng, 1), (twos,), 0, 1 << 20) % (slack + 1)
    sizes = sizes.at[1:1 + 2 * twos:2].set(donor - moved).at[2:2 + 2 * twos:2].set(taker + moved)
    return sizes[jax.random.permutation(jax.random.fold_in(rng, 2), amount)]


def scatter_about(own_key, extent, deviation, bound, shards=(), kind=jnp.bfloat16):
    drawn = deviation * jax.random.normal(own_key, extent, jnp.float32)
    if shards:
        drawn = drawn * block_scale(own_key, extent, shards, -0.22, 0.18)
    return jnp.clip(drawn, -bound, bound).astype(kind)


def setup_inputs(seed: int = 0) -> dict:
    seeds = jax.random.split(jax.random.key(seed), 10)
    return {
        "hidden": scatter_about(seeds[0], (PASSAGES, PASSAGE_LEN, D), 1.0, 6.0, ((0, 128),)),
        "norm_gain": jnp.clip(1.0 + 0.1 * jax.random.normal(seeds[1], (D,), jnp.float32), 0.5, 1.5),
        "w_qkv": scatter_about(seeds[2], (D, HEADS * HEAD_DIM + 2 * KV_HEADS * HEAD_DIM), D ** -0.5, 0.125, ((0, 16),)),
        "w_out": scatter_about(seeds[3], (HEADS * HEAD_DIM, D), (HEADS * HEAD_DIM) ** -0.5, 0.1875, ((0, 16),)),
        "final_gain": jnp.clip(1.0 + 0.1 * jax.random.normal(seeds[4], (D,), jnp.float32), 0.5, 1.5),
        "w_score": scatter_about(seeds[5], (D,), D ** -0.5, 0.125, (), jnp.float32),
        "prior": draw_prior(jax.random.fold_in(seeds[9], 71), 0),
        "labels": plant(jax.random.randint(seeds[7], (PASSAGES,), 0, 4), jax.random.fold_in(seeds[7], 1), 0, 3).astype(jnp.int32),
        "lengths": uneven(seeds[8], QUERIES, PASSAGES, LONGEST, 1).astype(jnp.int32),
    }


epsilon = 1e-05
loss_scale = 64.0

def forward_block(block, prior_part, norm_gain, w_qkv, w_out, final_gain, w_score):
    passages = block.shape[0]
    width_q = HEADS * HEAD_DIM
    width_k = KV_HEADS * HEAD_DIM
    ratio = HEADS // KV_HEADS
    values = block.astype(jnp.float32)
    mean_square = lax.optimization_barrier(jnp.mean(values * values, -1, keepdims=True))
    normal_rows = (values * lax.rsqrt(mean_square + epsilon) * norm_gain).astype(jnp.bfloat16)
    normal_rows = normal_rows.reshape(passages * PASSAGE_LEN, D)
    projected = jnp.dot(normal_rows, w_qkv, preferred_element_type=jnp.float32).astype(jnp.bfloat16)
    query_part = projected[:, :width_q].reshape(passages, PASSAGE_LEN, KV_HEADS, ratio, HEAD_DIM)
    key_part = projected[:, width_q:width_q + width_k].reshape(passages, PASSAGE_LEN, KV_HEADS, HEAD_DIM)
    value_part = projected[:, width_q + width_k:].reshape(passages, PASSAGE_LEN, KV_HEADS, HEAD_DIM)
    scores = jnp.einsum('bqgre,bkge->bgrqk', query_part.astype(jnp.float32), key_part.astype(jnp.float32)) * HEAD_DIM ** (-0.5)
    peak = lax.optimization_barrier(jnp.max(scores, -1, keepdims=True))
    expo = jnp.exp(scores - peak)
    probs = (expo / lax.optimization_barrier(jnp.sum(expo, -1, keepdims=True))).astype(jnp.bfloat16)
    attended = jnp.einsum('bgrqk,bkge->bqgre', probs.astype(jnp.float32), value_part.astype(jnp.float32)).astype(jnp.bfloat16)
    attended = attended.reshape(passages, PASSAGE_LEN, width_q)
    mixed = jnp.dot(attended.reshape(passages * PASSAGE_LEN, width_q), w_out, preferred_element_type=jnp.float32)
    residual = values + mixed.reshape(passages, PASSAGE_LEN, D)
    pooled = lax.optimization_barrier(jnp.mean(residual, 1))
    inverse = lax.rsqrt(lax.optimization_barrier(jnp.mean(pooled * pooled, -1, keepdims=True)) + epsilon)
    unit = pooled * inverse
    score = lax.optimization_barrier(jnp.sum(unit * final_gain * w_score, -1)) + prior_part
    return (score, normal_rows, query_part, key_part, value_part, probs, attended, unit, inverse)

def backward_block(saved, d_score, w_out, final_gain, w_score):
    score, normal_rows, query_part, key_part, value_part, probs, attended, unit, inverse = saved
    passages = attended.shape[0]
    d_unit = d_score[:, None] * w_score[None, :] * final_gain[None, :]
    d_pooled = inverse * (d_unit - unit * lax.optimization_barrier(jnp.mean(d_unit * unit, -1, keepdims=True)))
    d_rows = (d_pooled / PASSAGE_LEN).astype(jnp.bfloat16)
    attn_sum = lax.optimization_barrier(jnp.sum(attended, 1, dtype=jnp.float32)).astype(jnp.bfloat16)
    d_attended = jnp.dot(d_rows, w_out.T, preferred_element_type=jnp.float32).astype(jnp.bfloat16)
    d_heads = d_attended.reshape(passages, KV_HEADS, HEADS // KV_HEADS, HEAD_DIM).astype(jnp.float32)
    d_probs = jnp.einsum('bgre,bkge->bgrk', d_heads, value_part.astype(jnp.float32))
    probs_f = probs.astype(jnp.float32)
    inner = lax.optimization_barrier(jnp.sum(probs_f * d_probs[:, :, :, None, :], -1, keepdims=True))
    d_scores = (probs_f * (d_probs[:, :, :, None, :] - inner) * HEAD_DIM ** (-0.5)).astype(jnp.bfloat16)
    d_scores_f = d_scores.astype(jnp.float32)
    d_query = jnp.einsum('bgrqk,bkge->bqgre', d_scores_f, key_part.astype(jnp.float32)).astype(jnp.bfloat16)
    d_key = jnp.einsum('bgrqk,bqgre->bkge', d_scores_f, query_part.astype(jnp.float32)).astype(jnp.bfloat16)
    d_value = jnp.einsum('bgrqk,bgre->bkge', probs_f, d_heads).astype(jnp.bfloat16)
    rows = passages * PASSAGE_LEN
    d_projected = jnp.concatenate([d_query.reshape(rows, -1), d_key.reshape(rows, -1), d_value.reshape(rows, -1)], 1)
    term_qkv = jnp.dot(normal_rows.T, d_projected, preferred_element_type=jnp.float32)
    term_out = jnp.dot(attn_sum.T, d_rows, preferred_element_type=jnp.float32)
    return (term_qkv, term_out)

def reference(hidden, norm_gain, w_qkv, w_out, final_gain, w_score, prior, labels, lengths):
    devices = N_LIST * N_FSDP
    blocks = hidden.reshape(devices, PASSAGES_DEV, PASSAGE_LEN, D)
    prior_blocks = prior.reshape(devices, PASSAGES_DEV)

    def scores_only(operands):
        return forward_block(operands[0], operands[1], norm_gain, w_qkv, w_out, final_gain, w_score)[0]
    score = lax.map(scores_only, (blocks, prior_blocks)).reshape(PASSAGES)
    position = jnp.arange(PASSAGES, dtype=jnp.int32)
    ends = jnp.cumsum(lengths).astype(jnp.int32)
    owner = lax.optimization_barrier(jnp.sum((position[:, None] >= ends[None, :]).astype(jnp.int32), 1))
    member = (owner[:, None] == jnp.arange(QUERIES, dtype=jnp.int32)[None, :]).astype(jnp.float32)
    peak = lax.optimization_barrier(jnp.max(jnp.where(member > 0, score[:, None], -1e+30), 0))
    own_peak = lax.optimization_barrier(jnp.sum(member * peak[None, :], 1))
    total = lax.optimization_barrier(jnp.sum(member * jnp.exp(score - own_peak)[:, None], 0))
    label_weight = jnp.exp(labels.astype(jnp.float32))
    label_total = lax.optimization_barrier(jnp.sum(member * label_weight[:, None], 0))
    log_norm = peak + jnp.log(total)
    log_prob = score - lax.optimization_barrier(jnp.sum(member * log_norm[None, :], 1))
    target = label_weight / lax.optimization_barrier(jnp.sum(member * label_total[None, :], 1))
    loss = -loss_scale * jnp.sum(target * log_prob)
    d_score = loss_scale * (jnp.exp(log_prob) - target)
    d_blocks = d_score.reshape(devices, PASSAGES_DEV)

    def accumulate(carry, operands):
        block, prior_part, d_part = operands
        saved = forward_block(block, prior_part, norm_gain, w_qkv, w_out, final_gain, w_score)
        term_qkv, term_out = backward_block(saved, d_part, w_out, final_gain, w_score)
        term_qkv = lax.optimization_barrier(term_qkv.astype(jnp.bfloat16)).astype(jnp.float32)
        return ((carry[0] + term_qkv, carry[1] + term_out), None)
    start = (jnp.zeros(w_qkv.shape, jnp.float32), jnp.zeros(w_out.shape, jnp.float32))
    grads, _ = lax.scan(accumulate, start, (blocks, prior_blocks, d_blocks))
    return (loss, grads[0], grads[1])
```

```python
import functools

import jax
import jax.numpy as jnp
from jax import lax
from jax.experimental import pallas as pl
from jax.experimental.pallas import tpu as pltpu
from jax.sharding import Mesh
from jax.sharding import PartitionSpec as P

BF = jnp.bfloat16
F32 = jnp.float32
FSDP = ("x", "y")
LIST = ("z", "c")
ALL = ("z", "c", "x", "y")
EPS = 1e-05
SCALE = 64.0
TOKENS = 64
PASS = 16
ROWS = PASS * TOKENS
D = 2048
COLS = 1536
QW = 1024
KVW = 256
VMEM_CAP = 60 * 1024 * 1024


def mm(a, b, ca, cb):
    return lax.dot_general(a, b, (((ca,), (cb,)), ((), ())), preferred_element_type=F32)


def norm_rows(hidden, gain, normal, hsum):
    g = gain[...]

    @pl.loop(0, PASS)
    def _(p):
        at = pl.ds(pl.multiple_of(p * TOKENS, TOKENS), TOKENS)
        x = hidden[at, :].astype(F32)
        mean_square = jnp.mean(x * x, axis=1, keepdims=True)
        normal[at, :] = (x * lax.rsqrt(mean_square + EPS) * g).astype(BF)
        hsum[pl.ds(p, 1), :] = jnp.sum(x, axis=0, keepdims=True)


SIDES = (1, -1)


class Gather:
    def __init__(self, view, own, sems, across):
        self.view, self.own, self.sems, self.across = view, own, sems, across
        self.z, self.c, self.x, self.y = place()
        self.copies = {}

    def slot(self, half, near, far):
        dx, dy = (far, near) if half == 0 else (near, far)
        return (self.x + dx) % 4 * 4 + (self.y + dy) % 4

    def peer(self, half, stage, step):
        name = "yx"[(half + stage) % 2]
        return {name: ((self.y if name == "y" else self.x) + step) % 4}

    def go(self, key, src, dst, where):
        self.copies[key] = send(src, dst, self.sems, len(self.copies), where)

    def pass_on(self, half, near, far):
        slot = self.slot(half, near, far)
        if far == 0:
            for step in SIDES:
                ref = self.view(slot, half, None)
                self.go((half, 2, near, step), ref, ref, self.peer(half, 1, step))
        if self.across:
            ref = self.view(slot, half, None)
            self.go((half, 5, near, far), ref, ref, {"c": 1 - self.c})

    def relay(self, key, half, stage, slot, step):
        ref = self.view(slot, half, 0 if step == 1 else 1)
        self.go(key, ref, ref, self.peer(half, stage, step))

    def begin(self):
        for half in range(2):
            for stage, key in ((0, (half, 1)), (1, (half, 2, 0))):
                for step in SIDES:
                    self.go(
                        (*key, step),
                        self.own(half),
                        self.view(self.slot(half, 0, 0), half, None),
                        self.peer(half, stage, step),
                    )

    def near_sides(self):
        for half in range(2):
            for step in SIDES:
                self.copies[half, 1, step].wait_recv()
                self.relay((half, 3, step), half, 0, self.slot(half, -step, 0), step)
                self.pass_on(half, -step, 0)

    def near_opposite(self):
        for half in range(2):
            for step in SIDES:
                self.copies[half, 3, step].wait_recv()
            self.pass_on(half, 2, 0)

    def far_sides(self):
        for near in (0, 1, -1, 2):
            for half in range(2):
                for step in SIDES:
                    self.copies[half, 2, near, step].wait_recv()
                    slot = self.slot(half, near, -step)
                    self.relay((half, 4, near, step), half, 1, slot, step)
                    self.pass_on(half, near, -step)

    def far_opposite(self):
        for near in (0, 1, -1, 2):
            for half in range(2):
                for step in SIDES:
                    self.copies[half, 4, near, step].wait_recv()
                self.pass_on(half, near, 2)

    def across_sides(self):
        self.across_wait(lambda near, far: near != 2 and far != 2)

    def across_rest(self):
        self.across_wait(lambda near, far: near == 2 or far == 2)

    def across_wait(self, chosen):
        for key, copy in self.copies.items():
            if key[1] == 5 and chosen(key[2], key[3]):
                copy.wait_recv()

    def end(self):
        for copy in self.copies.values():
            copy.wait_send()


def plane_peers(x, y, c):
    return [{"x": (x + 1) % 4}, {"x": (x + 3) % 4}, {"y": (y + 1) % 4}, {"y": (y + 3) % 4}, {"c": 1 - c}]


def project_part(wt, normal, total, projected, slots, last):
    @pl.loop(0, 4)
    def _(n):
        at = pl.multiple_of(n * 256, 256)
        cols = [pl.ds(pl.multiple_of(s * 128, 128), 128) for s in slots]
        rhs = jnp.concatenate([normal[pl.ds(at, 256), col] for col in cols], axis=1)
        for m in range(2):
            rows = pl.ds(m * 768, 768)
            lhs = jnp.concatenate([wt[s, rows, :] for s in slots], axis=1)
            out = mm(lhs, rhs, 1, 1)
            if last:
                projected[rows, pl.ds(at, 256)] = (total[rows, pl.ds(at, 256)] + out).astype(BF)
            else:
                total[rows, pl.ds(at, 256)] = out


def project_body(hidden, gain, own, normal, hsum, projected, wt, total, send_sems, recv_sems):
    z, c, x, y = place()

    def rows_of(half, part):
        start, size = half * 384, 384
        if part is not None:
            start, size = start + part * 192, 192
        return pl.ds(pl.multiple_of(c * 768 + start, 64), size)

    gather = Gather(
        lambda slot, half, part: wt.at[slot, rows_of(half, part), :],
        lambda half: own.at[rows_of(half, None), :],
        (send_sems, recv_sems),
        True,
    )
    greet(plane_peers(x, y, c))
    gather.begin()
    wt[x * 4 + y] = own[...]
    norm_rows(hidden, gain, normal, hsum)
    gather.near_sides()
    gather.near_opposite()
    gather.far_sides()
    gather.across_sides()
    steps = [(0, 0), (0, 1), (0, -1), (1, 0), (-1, 0), (1, 1), (1, -1), (-1, 1)]
    early = [(x + i) % 4 * 4 + (y + j) % 4 for i, j in steps]
    every = [(i, j) for i in (0, 1, 2, -1) for j in (0, 1, 2, -1)]
    late = [(x + i) % 4 * 4 + (y + j) % 4 for i, j in every if (i, j) not in steps]
    project_part(wt, normal, total, projected, early, False)
    gather.far_opposite()
    gather.across_rest()
    project_part(wt, normal, total, projected, late, True)
    gather.end()


def halves_mask():
    return lax.broadcasted_iota(jnp.int32, (1, 512), 1) % 128 < 64


def side_by_side(block):
    return jnp.concatenate([block[r * 64 : (r + 1) * 64] for r in range(4)], axis=1)


def own_blocks(full, first):
    return jnp.where(first, full[:64], full[64:])


def both_blocks(part, first):
    zero = jnp.zeros_like(part)
    return jnp.concatenate([jnp.where(first, part, zero), jnp.where(first, zero, part)], axis=0)


def places(i):
    g, pair = i // 8, i % 8
    lanes = pl.ds(pl.multiple_of(pair * 128, 128), 128)
    q_rows = pl.ds(pl.multiple_of(g * 256, 256), 256)
    k_rows = pl.ds(pl.multiple_of(QW + g * 64, 64), 64)
    v_rows = pl.ds(pl.multiple_of(QW + KVW + g * 64, 64), 64)
    return g, lanes, q_rows, k_rows, v_rows


def segments():
    row = lax.broadcasted_iota(jnp.int32, (PASS, ROWS), 0)
    lane = lax.broadcasted_iota(jnp.int32, (PASS, ROWS), 1)
    return (lane // TOKENS == row).astype(F32).astype(BF)


def attend(projected, probs, attended, begin, end):
    @pl.loop(begin, end)
    def _(i):
        first = halves_mask()
        _, lanes, q_rows, k_rows, v_rows = places(i)
        q = side_by_side(projected[q_rows, lanes])
        k, v = projected[k_rows, lanes], projected[v_rows, lanes]
        scores = own_blocks(mm(k, q, 0, 0), first) * 0.125
        expo = jnp.exp(scores - jnp.max(scores, axis=0, keepdims=True))
        part = (expo * (1.0 / jnp.sum(expo, axis=0, keepdims=True))).astype(BF)
        probs[i] = part
        out = mm(v, both_blocks(part, first), 1, 0).astype(BF)
        for r in range(4):
            attended[pl.ds(pl.multiple_of(i // 8 * 256 + r * 64, 64), 64), lanes] = out[
                :, r * 128 : (r + 1) * 128
            ]


def attend_back(projected, probs, d_att, d_projected, begin, end):
    @pl.loop(begin, end)
    def _(i):
        first = halves_mask()
        g, lanes, q_rows, k_rows, v_rows = places(i)
        q = side_by_side(projected[q_rows, lanes])
        da = side_by_side(d_att[q_rows, lanes])
        k, v = projected[k_rows, lanes], projected[v_rows, lanes]
        part = probs[i]
        d_probs = own_blocks(mm(v, da, 0, 0), first)
        values = part.astype(F32)
        inner = jnp.sum(values * d_probs, axis=0, keepdims=True)
        d_scores = both_blocks((values * (d_probs - inner) * 0.125).astype(BF), first)
        dq = mm(k, d_scores, 1, 0).astype(BF)
        for r in range(4):
            d_projected[pl.ds(pl.multiple_of(g * 256 + r * 64, 64), 64), lanes] = dq[
                :, r * 128 : (r + 1) * 128
            ]
        d_projected[k_rows, lanes] = mm(q, d_scores, 1, 1).astype(BF)
        d_projected[v_rows, lanes] = mm(da, both_blocks(part, first), 1, 1).astype(BF)


def send(src, dst, sems, slot, where):
    copy = pltpu.make_async_remote_copy(
        src_ref=src,
        dst_ref=dst,
        send_sem=sems[0].at[slot],
        recv_sem=sems[1].at[slot],
        device_id=where,
        device_id_type=pl.DeviceIdType.MESH,
    )
    copy.start()
    return copy


def place():
    return tuple(lax.axis_index(a) for a in ALL)


def greet(peers):
    barrier = pltpu.get_barrier_semaphore()
    for where in peers:
        pl.semaphore_signal(barrier, inc=1, device_id=where, device_id_type=pl.DeviceIdType.MESH)
    pl.semaphore_wait(barrier, len(peers))


def axis_peers(name, at):
    return [{name: (at + j) % 4} for j in (1, 2, 3)]


def exchange(table, sems):
    z, c, x, y = place()
    group = z * 2 + c
    mine = (group * 4 + x) * 4 + y
    slot = 0
    for name, at, start, size in (
        ("y", y, mine, 1),
        ("x", x, mine - y, 4),
        ("c", c, group * 16, 16),
        ("z", z, z * 32, 32),
    ):
        peers = [{"c": 1 - c}] if name == "c" else axis_peers(name, at)
        block = table.at[pl.ds(start, size)]
        copies = [send(block, block, sems, slot + j, where) for j, where in enumerate(peers)]
        slot += len(peers)
        for copy in copies:
            copy.wait()


def listwise(table, lengths, mine):
    length_row = lengths[...].astype(F32)
    row = lax.broadcasted_iota(jnp.int32, (64, 64), 0)
    lane = lax.broadcasted_iota(jnp.int32, (64, 64), 1)
    ends = jnp.sum(jnp.where(lane <= row, length_row, 0.0), axis=1, keepdims=True)
    starts = jnp.sum(jnp.where(lane < row, length_row, 0.0), axis=1, keepdims=True)
    lanes = lax.broadcasted_iota(jnp.int32, (1, 128), 1).astype(F32)
    score, weight, member = [], [], []
    top = jnp.full((64, 128), -1e30, F32)
    labels = jnp.zeros((64, 128), F32)
    for r in range(16):
        both = table[8 * r]
        for j in range(1, 8):
            both = both + table[8 * r + j]
        score.append(both[:, :128])
        weight.append(both[:, 128:])
        position = lanes + 128.0 * r
        member.append(jnp.logical_and(position >= starts, position < ends))
        top = jnp.maximum(top, jnp.where(member[r], score[r], -1e30))
        labels = labels + jnp.where(member[r], weight[r], 0.0)
    peak = jnp.max(top, axis=1, keepdims=True)
    label_total = jnp.sum(labels, axis=1, keepdims=True)
    total = jnp.zeros((64, 128), F32)
    for r in range(16):
        total = total + jnp.exp(jnp.where(member[r], score[r] - peak, -1e30))
    log_norm = peak + jnp.log(jnp.sum(total, axis=1, keepdims=True))
    terms = jnp.zeros((1, 128), F32)
    own = jnp.zeros((1, 128), F32)
    for r in range(16):
        norm = jnp.sum(jnp.where(member[r], log_norm, 0.0), axis=0, keepdims=True)
        labels = jnp.sum(jnp.where(member[r], label_total, 0.0), axis=0, keepdims=True)
        log_prob = score[r] - norm
        target = weight[r] / labels
        terms = terms + target * log_prob
        d_score = SCALE * (jnp.exp(log_prob) - target)
        own = own + jnp.where(mine // 8 == r, d_score, 0.0)
    return -SCALE * jnp.sum(terms, axis=1, keepdims=True), own


def middle_body(
    projected, hsum, own, final_gain, w_score, prior, labels, lengths,
    probs, pair, d_att, loss,
    attended, blocks, table, send_sems, recv_sems, out_send_sems, out_recv_sems,
):
    z, c, x, y = place()

    def rows_of(half):
        return pl.ds(pl.multiple_of(c * 32 + half * 16, 16), 16)

    def cols_of(part):
        return pl.ds(0, 2048) if part is None else pl.ds(part * 1024, 1024)

    gather = Gather(
        lambda slot, half, part: blocks.at[slot, rows_of(half), cols_of(part)],
        lambda half: own.at[rows_of(half), :],
        (out_send_sems, out_recv_sems),
        True,
    )
    greet(axis_peers("y", y) + axis_peers("x", x) + [{"c": 1 - c}] + axis_peers("z", z))
    gather.begin()
    blocks[x * 4 + y] = own[...]
    attend(projected, probs, attended, 0, 8)
    gather.near_sides()
    attend(projected, probs, attended, 8, 16)
    gather.near_opposite()
    attend(projected, probs, attended, 16, 24)
    gather.far_sides()
    attend(projected, probs, attended, 24, 32)
    gather.far_opposite()
    gather.across_sides()
    gather.across_rest()
    w_out = blocks[...].reshape(QW, D)
    sums = mm(segments(), attended[...], 1, 1)
    high = sums.astype(BF)
    pair[:, D:] = high
    low = (sums - high.astype(F32)).astype(BF)
    mixed = mm(jnp.concatenate([high, low], axis=0), w_out, 1, 0)
    pooled = (hsum[...] + mixed[:16] + mixed[16:]) * (1.0 / TOKENS)
    inverse = lax.rsqrt(jnp.mean(pooled * pooled, axis=1, keepdims=True) + EPS)
    unit = pooled * inverse
    weight = final_gain[...] * w_score[...]
    score = jnp.sum(unit * weight, axis=1, keepdims=True) + prior[...]
    mine = ((z * 2 + c) * 4 + x) * 4 + y
    row = lax.broadcasted_iota(jnp.int32, (16, 128), 0)
    lane = lax.broadcasted_iota(jnp.int32, (16, 128), 1)
    here = lane == row + mine % 8 * 16
    label_weight = jnp.exp(labels[...].astype(F32))
    score_row = jnp.sum(jnp.where(here, score, 0.0), axis=0, keepdims=True)
    label_row = jnp.sum(jnp.where(here, label_weight, 0.0), axis=0, keepdims=True)
    table[mine] = jnp.concatenate([score_row, label_row], axis=1)
    exchange(table, (send_sems, recv_sems))
    loss_value, own = listwise(table, lengths, mine)
    loss[...] = loss_value
    d_score = jnp.sum(jnp.where(here, own, 0.0), axis=1, keepdims=True)
    d_unit = d_score * weight
    d_pooled = inverse * (d_unit - unit * jnp.mean(d_unit * unit, axis=1, keepdims=True))
    grads = (d_pooled * (1.0 / TOKENS)).astype(BF)
    pair[:, :D] = grads
    d_attended = mm(w_out, grads, 1, 1).astype(BF)
    d_att[...] = mm(d_attended, segments(), 1, 0).astype(BF)
    gather.end()


ORDER = (2, 1, -1, 0)


class Scatter:
    def __init__(self, blocks, slabs, first, second, third, fourth, sems):
        self.blocks, self.slabs, self.sems = blocks, slabs, sems
        self.first, self.second, self.third, self.fourth = first, second, third, fourth
        self.z, self.c, self.x, self.y = place()
        self.copies = {}

    def at(self, half, stage):
        return self.x if (half + stage) % 2 == 0 else self.y

    def go(self, key, src, dst, half, stage, step):
        name = "xy"[(half + stage) % 2]
        where = {name: (self.at(half, stage) + step) % 4}
        self.copies[key] = send(src, dst, self.sems, len(self.copies), where)

    def part(self, step):
        return pl.ds(0 if step == 1 else 192, 192)

    def wide_first(self, half):
        block = self.blocks.at[half, 2]
        for k, step in enumerate(SIDES):
            self.go((half, 1, step), block.at[:, self.part(step), :], self.first.at[half, k], half, 0, step)

    def wide_second(self, half, step):
        k = SIDES.index(step)
        self.copies[half, 1, step].wait_recv()
        rows = self.part(step)
        at = step % 4
        mine = self.blocks[half, at, :, rows, :].astype(F32)
        self.blocks[half, at, :, rows, :] = (mine + self.first[half, k].astype(F32)).astype(BF)
        self.go((half, 2, step), self.blocks.at[half, at], self.second.at[half, k], half, 0, step)

    def wide_last(self, half):
        total = self.blocks[half, 0].astype(F32)
        for k, step in enumerate(SIDES):
            self.copies[half, 2, step].wait_recv()
            total = total + self.second[half, k].astype(F32)
        self.slabs[half] = total.astype(BF)
        slab = self.slabs.at[half, (self.at(half, 1) + 2) % 4]
        for k, step in enumerate(SIDES):
            self.go((half, 3, step), slab.at[self.part(step), :], self.third.at[half, k], half, 1, step)

    def narrow_second(self, half):
        for k, step in enumerate(SIDES):
            self.copies[half, 3, step].wait_recv()
            rows = self.part(step)
            at = (self.at(half, 1) + step) % 4
            mine = self.slabs[half, at, rows, :].astype(F32)
            self.slabs[half, at, rows, :] = (mine + self.third[half, k].astype(F32)).astype(BF)
            self.go((half, 4, step), self.slabs.at[half, at], self.fourth.at[half, k], half, 1, step)

    def narrow_last(self, half):
        total = self.slabs[half, self.at(half, 1)].astype(F32)
        for k, step in enumerate(SIDES):
            self.copies[half, 4, step].wait_recv()
            total = total + self.fourth[half, k].astype(F32)
        return total

    def end(self):
        for copy in self.copies.values():
            copy.wait_send()


def outer_peers(z, c):
    return [
        {"z": (z + j) % 4, "c": (c + k) % 2} for j in range(4) for k in range(2) if (j, k) != (0, 0)
    ]


def gradient_body(
    projected, probs, d_att, normal, pair,
    grad_qkv, grad_out,
    d_projected, everyone, wide, outer, outer_in,
    leaving, arriving, blocks, slabs, first, second, third, fourth, layers, layers_in,
    pair_send, pair_recv, core_send, core_recv, ring_send, ring_recv, list_send, list_recv,
):
    z, c, x, y = place()

    def lanes_of(half, part):
        return pl.ds(half * 1536, 1536) if part is None else pl.ds(half * 1536 + part * 768, 768)

    gather = Gather(
        lambda slot, half, part: everyone.at[slot, :, lanes_of(half, part)],
        lambda half: pair.at[:, lanes_of(half, None)],
        (pair_send, pair_recv),
        False,
    )
    outers = outer_peers(z, c)
    greet(plane_peers(x, y, c)[:4] + outers)
    gather.begin()
    everyone[x * 4 + y] = pair[...]
    attend_back(projected, probs, d_att, d_projected, 0, 8)
    gather.near_sides()
    attend_back(projected, probs, d_att, d_projected, 8, 16)
    gather.near_opposite()
    attend_back(projected, probs, d_att, d_projected, 16, 24)
    gather.far_sides()
    attend_back(projected, probs, d_att, d_projected, 24, 32)
    gather.far_opposite()

    ring = Scatter(blocks, slabs, first, second, third, fourth, (ring_send, ring_recv))
    units = [(step, half) for step in ORDER for half in range(2)]
    swaps = {}

    def unit(step, half):
        if half == 0:
            start = pl.multiple_of((x + step) % 4 * 512, 512)
            rhs = normal[:, pl.ds(start, 512)]
        else:
            at = [pl.multiple_of((i * 4 + (y + step) % 4) * 128, 128) for i in range(4)]
            rhs = jnp.concatenate([normal[:, pl.ds(a, 128)] for a in at], axis=1)
        for parity, target in ((1 - c, leaving), (c, blocks)):
            starts = [pl.multiple_of((4 * half + 2 * i + parity) * 192, 64) for i in range(2)]
            lhs = jnp.concatenate([d_projected[pl.ds(s, 192), :] for s in starts], axis=0)
            out = mm(lhs, rhs, 1, 0).astype(BF)
            for j in range(4):
                target[half, step % 4, j] = out[:, j * 128 : (j + 1) * 128]
        swaps[step, half] = send(
            leaving.at[half, step % 4],
            arriving.at[half, step % 4],
            (core_send, core_recv),
            len(swaps),
            {"c": 1 - c},
        )

    def joined(step, half):
        swaps[step, half].wait_recv()
        at = step % 4
        mine = blocks[half, at].astype(F32)
        blocks[half, at] = (mine + arriving[half, at].astype(F32)).astype(BF)

    for n, (step, half) in enumerate(units):
        unit(step, half)
        if n:
            joined(*units[n - 1])
            if units[n - 1][0] == 2:
                ring.wide_first(units[n - 1][1])
        if n == 5:
            ring.wide_second(0, 1)
        if n == 6:
            ring.wide_second(1, 1)
            ring.wide_second(0, -1)
    joined(*units[-1])
    ring.wide_second(1, -1)

    f = x * 4 + y
    lanes = pl.ds(pl.multiple_of(D + f // 2 * 128, 128), 128)
    sums = everyone[:, :, lanes].reshape(256, 128)
    wide[...] = mm(sums, everyone[:, :, :D].reshape(256, D), 0, 0)
    mine = wide[pl.ds(pl.multiple_of(f % 2 * 64, 64), 64), :].astype(BF)
    for l in range(8):
        outer[l] = mine[:, l * 256 : (l + 1) * 256]
    out_copies = [
        send(outer.at[w["z"] * 2 + w["c"]], outer_in.at[k], (list_send, list_recv), k, w)
        for k, w in enumerate(outers)
    ]
    ring.wide_last(0)
    ring.wide_last(1)
    ring.narrow_second(0)
    ring.narrow_second(1)
    total = outer[z * 2 + c].astype(F32)
    for k, copy in enumerate(out_copies):
        copy.wait()
        total = total + outer_in[k].astype(F32)
    grad_out[...] = total
    for half in range(2):
        both = ring.narrow_last(half).astype(BF)
        layers[2 * half] = both[:192]
        layers[2 * half + 1] = both[192:]
    layer_copies = [
        send(layers.at[(z + j) % 4], layers_in.at[j - 1], (list_send, list_recv), 6 + j, {"z": (z + j) % 4})
        for j in (1, 2, 3)
    ]
    total = layers[z].astype(F32)
    for k, copy in enumerate(layer_copies):
        copy.wait()
        total = total + layers_in[k].astype(F32)
    grad_qkv[...] = total
    gather.end()
    ring.end()
    for copy in swaps.values():
        copy.wait_send()


def vm():
    return pl.BlockSpec(memory_space=pltpu.VMEM)


def shape(*dims, dtype=BF):
    return jax.ShapeDtypeStruct(dims, dtype)


def semaphores(count):
    return [pltpu.SemaphoreType.DMA((count,))] * 2


def local(hidden, norm_gain, w_qkv, w_out, final_gain, w_score, prior, labels, lengths):
    rows = hidden.reshape(ROWS, D)
    params = functools.partial(
        pltpu.CompilerParams, vmem_limit_bytes=VMEM_CAP, has_side_effects=True
    )
    normal, hsum, projected = pl.pallas_call(
        project_body,
        out_shape=(shape(ROWS, D), shape(PASS, D, dtype=F32), shape(COLS, ROWS)),
        in_specs=[vm()] * 3,
        out_specs=(vm(),) * 3,
        scratch_shapes=[pltpu.VMEM((16, COLS, 128), BF), pltpu.VMEM((COLS, ROWS), F32)]
        + semaphores(70),
        compiler_params=params(collective_id=0),
        name="project",
    )(rows, norm_gain.reshape(1, D), w_qkv.T)
    probs, pair, d_att, loss = pl.pallas_call(
        middle_body,
        out_shape=(
            shape(32, 64, 512),
            shape(PASS, D + QW),
            shape(QW, ROWS),
            shape(1, 1, dtype=F32),
        ),
        in_specs=[vm()] * 8,
        out_specs=(vm(),) * 4,
        scratch_shapes=[
            pltpu.VMEM((QW, ROWS), BF),
            pltpu.VMEM((16, 64, D), BF),
            pltpu.VMEM((128, 1, 256), F32),
        ]
        + semaphores(10)
        + semaphores(70),
        compiler_params=params(collective_id=1),
        name="middle",
    )(
        projected, hsum, w_out, final_gain.reshape(1, D), w_score.reshape(1, D),
        prior.reshape(PASS, 1), labels.reshape(PASS, 1), lengths.reshape(1, -1),
    )
    grad_qkv, grad_out = pl.pallas_call(
        gradient_body,
        out_shape=(shape(192, 128, dtype=F32), shape(64, 256, dtype=F32)),
        in_specs=[vm()] * 5,
        out_specs=(vm(),) * 2,
        scratch_shapes=[
            pltpu.VMEM((COLS, ROWS), BF),
            pltpu.VMEM((16, PASS, D + QW), BF),
            pltpu.VMEM((128, D), F32),
            pltpu.VMEM((8, 64, 256), BF),
            pltpu.VMEM((7, 64, 256), BF),
            pltpu.VMEM((2, 4, 4, 384, 128), BF),
            pltpu.VMEM((2, 4, 4, 384, 128), BF),
            pltpu.VMEM((2, 4, 4, 384, 128), BF),
            pltpu.VMEM((2, 4, 384, 128), BF),
            pltpu.VMEM((2, 2, 4, 192, 128), BF),
            pltpu.VMEM((2, 2, 4, 384, 128), BF),
            pltpu.VMEM((2, 2, 192, 128), BF),
            pltpu.VMEM((2, 2, 384, 128), BF),
            pltpu.VMEM((4, 192, 128), BF),
            pltpu.VMEM((3, 192, 128), BF),
        ]
        + semaphores(40)
        + semaphores(8)
        + semaphores(16)
        + semaphores(10),
        compiler_params=params(collective_id=2),
        name="gradient",
    )(projected, probs, d_att, normal, pair)
    return loss.reshape(()), grad_qkv.T, grad_out


def solution(mesh):
    torus = Mesh(mesh.devices.reshape(4, 2, 4, 4), ALL)
    in_specs = (
        P(ALL, None, None), P(), P(FSDP, None), P(FSDP, None), P(), P(), P(ALL), P(ALL), P(),
    )
    out_specs = (P(), P(FSDP, LIST), P(FSDP, LIST))
    return jax.shard_map(local, mesh=torus, in_specs=in_specs, out_specs=out_specs, check_vma=False)
```

```python
import jax
import jax.numpy as jnp
from jax import lax
from jax.experimental import pallas as pl
from jax.experimental.pallas import tpu as pltpu
from jax.sharding import Mesh
from jax.sharding import PartitionSpec as P

BF = jnp.bfloat16
F32 = jnp.float32
FSDP = ("x", "y")
LIST = ("z", "c")
ALL = ("z", "c", "x", "y")
EPS = 1e-05
SCALE = 64.0
TOKENS = 64
PASS = 16
ROWS = PASS * TOKENS
D = 2048
COLS = 1536
QW = 1024
KVW = 256
VMEM_CAP = 63 * 1024 * 1024


def mm(a, b, ca, cb):
    return lax.dot_general(a, b, (((ca,), (cb,)), ((), ())), preferred_element_type=F32)


def norm_rows(hidden, gain, normal, hsum):
    g = gain[...]

    @pl.loop(0, PASS)
    def _(p):
        at = pl.ds(pl.multiple_of(p * TOKENS, TOKENS), TOKENS)
        x = hidden[at, :].astype(F32)
        mean_square = jnp.mean(x * x, axis=1, keepdims=True)
        normal[at, :] = (x * lax.rsqrt(mean_square + EPS) * g).astype(BF)
        hsum[pl.ds(p, 1), :] = jnp.sum(x, axis=0, keepdims=True)


SIDES = (1, -1)


class Gather:
    def __init__(self, view, own, sems, across):
        self.view, self.own, self.sems, self.across = view, own, sems, across
        self.z, self.c, self.x, self.y = place()
        self.copies = {}

    def slot(self, half, near, far):
        dx, dy = (far, near) if half == 0 else (near, far)
        return (self.x + dx) % 4 * 4 + (self.y + dy) % 4

    def peer(self, half, stage, step):
        name = "yx"[(half + stage) % 2]
        return {name: ((self.y if name == "y" else self.x) + step) % 4}

    def go(self, key, src, dst, where):
        self.copies[key] = send(src, dst, self.sems, len(self.copies), where)

    def pass_on(self, half, near, far):
        slot = self.slot(half, near, far)
        if far == 0:
            for step in SIDES:
                ref = self.view(slot, half, None)
                self.go((half, 2, near, step), ref, ref, self.peer(half, 1, step))
        if self.across:
            ref = self.view(slot, half, None)
            self.go((half, 5, near, far), ref, ref, {"c": 1 - self.c})

    def relay(self, key, half, stage, slot, step):
        ref = self.view(slot, half, 0 if step == 1 else 1)
        self.go(key, ref, ref, self.peer(half, stage, step))

    def begin(self):
        for half in range(2):
            for stage, key in ((0, (half, 1)), (1, (half, 2, 0))):
                for step in SIDES:
                    self.go(
                        (*key, step),
                        self.own(half),
                        self.view(self.slot(half, 0, 0), half, None),
                        self.peer(half, stage, step),
                    )

    def near_sides(self):
        for half in range(2):
            for step in SIDES:
                self.copies[half, 1, step].wait_recv()
                self.relay((half, 3, step), half, 0, self.slot(half, -step, 0), step)
                self.pass_on(half, -step, 0)

    def near_opposite(self):
        for half in range(2):
            for step in SIDES:
                self.copies[half, 3, step].wait_recv()
            self.pass_on(half, 2, 0)

    def far_sides(self):
        for near in (0, 1, -1, 2):
            for half in range(2):
                for step in SIDES:
                    self.copies[half, 2, near, step].wait_recv()
                    slot = self.slot(half, near, -step)
                    self.relay((half, 4, near, step), half, 1, slot, step)
                    self.pass_on(half, near, -step)

    def far_opposite(self):
        for near in (0, 1, -1, 2):
            for half in range(2):
                for step in SIDES:
                    self.copies[half, 4, near, step].wait_recv()
                self.pass_on(half, near, 2)

    def across_sides(self):
        self.across_wait(lambda near, far: near != 2 and far != 2)

    def across_rest(self):
        self.across_wait(lambda near, far: near == 2 or far == 2)

    def across_wait(self, chosen):
        for key, copy in self.copies.items():
            if key[1] == 5 and chosen(key[2], key[3]):
                copy.wait_recv()

    def end(self):
        for copy in self.copies.values():
            copy.wait_send()


def plane_peers(x, y, c):
    return [{"x": (x + 1) % 4}, {"x": (x + 3) % 4}, {"y": (y + 1) % 4}, {"y": (y + 3) % 4}, {"c": 1 - c}]


def project_part(wt, normal, total, projected, slots, last):
    @pl.loop(0, 4)
    def _(n):
        at = pl.multiple_of(n * 256, 256)
        cols = [pl.ds(pl.multiple_of(s * 128, 128), 128) for s in slots]
        rhs = jnp.concatenate([normal[pl.ds(at, 256), col] for col in cols], axis=1)
        for m in range(2):
            rows = pl.ds(m * 768, 768)
            lhs = jnp.concatenate([wt[s, rows, :] for s in slots], axis=1)
            out = mm(lhs, rhs, 1, 1)
            if last:
                projected[rows, pl.ds(at, 256)] = (total[rows, pl.ds(at, 256)] + out).astype(BF)
            else:
                total[rows, pl.ds(at, 256)] = out


def halves_mask():
    return lax.broadcasted_iota(jnp.int32, (1, 512), 1) % 128 < 64


def side_by_side(block):
    return jnp.concatenate([block[r * 64 : (r + 1) * 64] for r in range(4)], axis=1)


def own_blocks(full, first):
    return jnp.where(first, full[:64], full[64:])


def both_blocks(part, first):
    zero = jnp.zeros_like(part)
    return jnp.concatenate([jnp.where(first, part, zero), jnp.where(first, zero, part)], axis=0)


def places(i):
    g, pair = i // 8, i % 8
    lanes = pl.ds(pl.multiple_of(pair * 128, 128), 128)
    q_rows = pl.ds(pl.multiple_of(g * 256, 256), 256)
    k_rows = pl.ds(pl.multiple_of(QW + g * 64, 64), 64)
    v_rows = pl.ds(pl.multiple_of(QW + KVW + g * 64, 64), 64)
    return g, lanes, q_rows, k_rows, v_rows


def segments():
    row = lax.broadcasted_iota(jnp.int32, (PASS, ROWS), 0)
    lane = lax.broadcasted_iota(jnp.int32, (PASS, ROWS), 1)
    return (lane // TOKENS == row).astype(F32).astype(BF)


def attend(projected, probs, attended, begin, end):
    @pl.loop(begin, end)
    def _(i):
        first = halves_mask()
        _, lanes, q_rows, k_rows, v_rows = places(i)
        q = side_by_side(projected[q_rows, lanes])
        k, v = projected[k_rows, lanes], projected[v_rows, lanes]
        scores = own_blocks(mm(k, q, 0, 0), first) * 0.125
        expo = jnp.exp(scores - jnp.max(scores, axis=0, keepdims=True))
        part = (expo * (1.0 / jnp.sum(expo, axis=0, keepdims=True))).astype(BF)
        probs[i] = part
        out = mm(v, both_blocks(part, first), 1, 0).astype(BF)
        for r in range(4):
            attended[pl.ds(pl.multiple_of(i // 8 * 256 + r * 64, 64), 64), lanes] = out[
                :, r * 128 : (r + 1) * 128
            ]


def attend_back(projected, probs, d_att, d_projected, begin, end):
    @pl.loop(begin, end)
    def _(i):
        first = halves_mask()
        g, lanes, q_rows, k_rows, v_rows = places(i)
        q = side_by_side(projected[q_rows, lanes])
        da = side_by_side(d_att[q_rows, lanes])
        k, v = projected[k_rows, lanes], projected[v_rows, lanes]
        part = probs[i]
        d_probs = own_blocks(mm(v, da, 0, 0), first)
        values = part.astype(F32)
        inner = jnp.sum(values * d_probs, axis=0, keepdims=True)
        d_scores = both_blocks((values * (d_probs - inner) * 0.125).astype(BF), first)
        dq = mm(k, d_scores, 1, 0).astype(BF)
        for r in range(4):
            d_projected[pl.ds(pl.multiple_of(g * 256 + r * 64, 64), 64), lanes] = dq[
                :, r * 128 : (r + 1) * 128
            ]
        d_projected[k_rows, lanes] = mm(q, d_scores, 1, 1).astype(BF)
        d_projected[v_rows, lanes] = mm(da, both_blocks(part, first), 1, 1).astype(BF)


def send(src, dst, sems, slot, where):
    copy = pltpu.make_async_remote_copy(
        src_ref=src,
        dst_ref=dst,
        send_sem=sems[0].at[slot],
        recv_sem=sems[1].at[slot],
        device_id=where,
        device_id_type=pl.DeviceIdType.MESH,
    )
    copy.start()
    return copy


def place():
    return tuple(lax.axis_index(a) for a in ALL)


def greet(peers):
    barrier = pltpu.get_barrier_semaphore()
    for where in peers:
        pl.semaphore_signal(barrier, inc=1, device_id=where, device_id_type=pl.DeviceIdType.MESH)
    pl.semaphore_wait(barrier, len(peers))


def axis_peers(name, at):
    return [{name: (at + j) % 4} for j in (1, 2, 3)]


class Exchange:
    def __init__(self, table, sems):
        z, c, x, y = place()
        group = z * 2 + c
        mine = (group * 4 + x) * 4 + y
        self.table, self.sems, self.used, self.copies = table, sems, 0, []
        self.stages = [
            (axis_peers("y", y), mine, 1),
            (axis_peers("x", x), mine - y, 4),
            ([{"c": 1 - c}], group * 16, 16),
            (axis_peers("z", z), z * 32, 32),
        ]

    def start(self, stage):
        peers, start, size = self.stages[stage]
        block = self.table.at[pl.ds(start, size)]
        self.copies = [send(block, block, self.sems, self.used + j, w) for j, w in enumerate(peers)]
        self.used += len(peers)

    def wait(self):
        for copy in self.copies:
            copy.wait()


def listwise(table, lengths, group):
    length_row = lengths[...].astype(F32)
    row = lax.broadcasted_iota(jnp.int32, (64, 64), 0)
    lane = lax.broadcasted_iota(jnp.int32, (64, 64), 1)
    ends = jnp.sum(jnp.where(lane <= row, length_row, 0.0), axis=1, keepdims=True)
    starts = jnp.sum(jnp.where(lane < row, length_row, 0.0), axis=1, keepdims=True)
    lanes = lax.broadcasted_iota(jnp.int32, (1, 128), 1).astype(F32)
    score, weight, member = [], [], []
    top = jnp.full((64, 128), -1e30, F32)
    labels = jnp.zeros((64, 128), F32)
    for r in range(16):
        both = table[8 * r]
        for j in range(1, 8):
            both = both + table[8 * r + j]
        score.append(both[:, :128])
        weight.append(both[:, 128:])
        position = lanes + 128.0 * r
        member.append(jnp.logical_and(position >= starts, position < ends))
        top = jnp.maximum(top, jnp.where(member[r], score[r], -1e30))
        labels = labels + jnp.where(member[r], weight[r], 0.0)
    peak = jnp.max(top, axis=1, keepdims=True)
    label_total = jnp.sum(labels, axis=1, keepdims=True)
    total = jnp.zeros((64, 128), F32)
    for r in range(16):
        total = total + jnp.exp(jnp.where(member[r], score[r] - peak, -1e30))
    log_norm = peak + jnp.log(jnp.sum(total, axis=1, keepdims=True))
    terms = jnp.zeros((1, 128), F32)
    own = [jnp.zeros((1, 128), F32)] * 2
    for r in range(16):
        norm = jnp.sum(jnp.where(member[r], log_norm, 0.0), axis=0, keepdims=True)
        labels = jnp.sum(jnp.where(member[r], label_total, 0.0), axis=0, keepdims=True)
        log_prob = score[r] - norm
        target = weight[r] / labels
        terms = terms + target * log_prob
        d_score = SCALE * (jnp.exp(log_prob) - target)
        own[r % 2] = own[r % 2] + jnp.where(group == r // 2, d_score, 0.0)
    return -SCALE * jnp.sum(terms, axis=1, keepdims=True), own


ORDER = (2, 1, -1, 0)


class Scatter:
    def __init__(self, blocks, slabs, first, second, third, fourth, sems):
        self.blocks, self.slabs, self.sems = blocks, slabs, sems
        self.first, self.second, self.third, self.fourth = first, second, third, fourth
        self.z, self.c, self.x, self.y = place()
        self.copies = {}

    def at(self, half, stage):
        return self.x if (half + stage) % 2 == 0 else self.y

    def go(self, key, src, dst, half, stage, step):
        name = "xy"[(half + stage) % 2]
        where = {name: (self.at(half, stage) + step) % 4}
        self.copies[key] = send(src, dst, self.sems, len(self.copies), where)

    def part(self, step):
        return pl.ds(0 if step == 1 else 192, 192)

    def wide_first(self, half):
        block = self.blocks.at[half, 2]
        for k, step in enumerate(SIDES):
            self.go((half, 1, step), block.at[:, self.part(step), :], self.first.at[half, k], half, 0, step)

    def wide_second(self, half, step):
        k = SIDES.index(step)
        self.copies[half, 1, step].wait_recv()
        rows = self.part(step)
        at = step % 4
        mine = self.blocks[half, at, :, rows, :].astype(F32)
        self.blocks[half, at, :, rows, :] = (mine + self.first[half, k].astype(F32)).astype(BF)
        self.go((half, 2, step), self.blocks.at[half, at], self.second.at[half, k], half, 0, step)

    def wide_last(self, half):
        total = self.blocks[half, 0].astype(F32)
        for k, step in enumerate(SIDES):
            self.copies[half, 2, step].wait_recv()
            total = total + self.second[half, k].astype(F32)
        self.slabs[half] = total.astype(BF)
        slab = self.slabs.at[half, (self.at(half, 1) + 2) % 4]
        for k, step in enumerate(SIDES):
            self.go((half, 3, step), slab.at[self.part(step), :], self.third.at[half, k], half, 1, step)

    def narrow_second(self, half):
        for k, step in enumerate(SIDES):
            self.copies[half, 3, step].wait_recv()
            rows = self.part(step)
            at = (self.at(half, 1) + step) % 4
            mine = self.slabs[half, at, rows, :].astype(F32)
            self.slabs[half, at, rows, :] = (mine + self.third[half, k].astype(F32)).astype(BF)
            self.go((half, 4, step), self.slabs.at[half, at], self.fourth.at[half, k], half, 1, step)

    def narrow_last(self, half):
        total = self.slabs[half, self.at(half, 1)].astype(F32)
        for k, step in enumerate(SIDES):
            self.copies[half, 4, step].wait_recv()
            total = total + self.fourth[half, k].astype(F32)
        return total

    def end(self):
        for copy in self.copies.values():
            copy.wait_send()


def outer_peers(z, c):
    return [
        {"z": (z + j) % 4, "c": (c + k) % 2} for j in range(4) for k in range(2) if (j, k) != (0, 0)
    ]


def as_column(row):
    count = row.shape[1]
    same = lax.broadcasted_iota(jnp.int32, (count, count), 0) == lax.broadcasted_iota(
        jnp.int32, (count, count), 1
    )
    return jnp.sum(jnp.where(same, row, 0.0), axis=1, keepdims=True)


def whole_body(
    hidden, gain, w_qkv, w_out_own, final_gain, w_score, prior, labels, lengths,
    loss, grad_qkv, grad_out,
    normal, hsum, wt, total_f, projected, probs, attended, w_blocks, table, pair,
    d_projected, everyone, wide, outer, outer_in,
    leaving, arriving, blocks, slabs, first, second, third, fourth, layers, layers_in,
    qkv_send, qkv_recv, out_send, out_recv, table_send, table_recv,
    pair_send, pair_recv, core_send, core_recv, ring_send, ring_recv, list_send, list_recv,
):
    z, c, x, y = place()
    d_att = attended
    f = x * 4 + y
    group = z * 2 + c

    def qkv_rows(half, part, core):
        start, size = half * 384, 384
        if part is not None:
            start, size = start + part * 192, 192
        return pl.ds(pl.multiple_of(core * 768 + start, 64), size)

    def out_rows(half):
        return pl.ds(pl.multiple_of(c * 32 + half * 16, 16), 16)

    def out_cols(part):
        return pl.ds(0, D) if part is None else pl.ds(part * 1024, 1024)

    def pair_cols(half, part):
        return pl.ds(half * 1536, 1536) if part is None else pl.ds(half * 1536 + part * 768, 768)

    qkv_gather = Gather(
        lambda slot, half, part: wt.at[slot, qkv_rows(half, part, c), :],
        lambda half: wt.at[f, qkv_rows(half, None, c), :],
        (qkv_send, qkv_recv),
        True,
    )
    out_gather = Gather(
        lambda slot, half, part: w_blocks.at[slot, out_rows(half), out_cols(part)],
        lambda half: w_out_own.at[out_rows(half), :],
        (out_send, out_recv),
        True,
    )
    pair_gather = Gather(
        lambda slot, half, part: everyone.at[slot, :, pair_cols(half, part)],
        lambda half: pair.at[:, pair_cols(half, None)],
        (pair_send, pair_recv),
        False,
    )
    scores = Exchange(table, (table_send, table_recv))
    outers = outer_peers(z, c)

    def turned(core):
        for half in range(2):
            cols = pl.ds(pl.multiple_of(core * 768 + half * 384, 128), 384)
            wt[f, qkv_rows(half, None, core), :] = w_qkv[:, cols].T

    turned(c)
    greet(axis_peers("y", y) + axis_peers("x", x) + outers)
    qkv_gather.begin()
    turned(1 - c)
    w_blocks[f] = w_out_own[...]
    norm_rows(hidden, gain, normal, hsum)
    qkv_gather.near_sides()
    qkv_gather.near_opposite()
    qkv_gather.far_sides()
    out_gather.begin()
    qkv_gather.across_sides()
    steps = [(0, 0), (0, 1), (0, -1), (1, 0), (-1, 0), (1, 1), (1, -1), (-1, 1)]
    early = [(x + i) % 4 * 4 + (y + j) % 4 for i, j in steps]
    every = [(i, j) for i in (0, 1, 2, -1) for j in (0, 1, 2, -1)]
    late = [(x + i) % 4 * 4 + (y + j) % 4 for i, j in every if (i, j) not in steps]
    project_part(wt, normal, total_f, projected, early, False)
    qkv_gather.far_opposite()
    out_gather.near_sides()
    qkv_gather.across_rest()
    project_part(wt, normal, total_f, projected, late, True)
    out_gather.near_opposite()
    attend(projected, probs, attended, 0, 8)
    out_gather.far_sides()
    attend(projected, probs, attended, 8, 24)
    out_gather.far_opposite()
    attend(projected, probs, attended, 24, 32)
    out_gather.across_sides()
    out_gather.across_rest()

    w_out = w_blocks[...].reshape(QW, D)
    sums = mm(segments(), attended[...], 1, 1)
    high = sums.astype(BF)
    low = (sums - high.astype(F32)).astype(BF)
    mixed = mm(jnp.concatenate([high, low], axis=0), w_out, 1, 0)
    pooled = (hsum[...] + mixed[:16] + mixed[16:]) * (1.0 / TOKENS)
    inverse = lax.rsqrt(jnp.mean(pooled * pooled, axis=1, keepdims=True) + EPS)
    unit = pooled * inverse
    weight = final_gain[...] * w_score[...]
    score = jnp.sum(unit * weight, axis=1, keepdims=True) + as_column(prior[...])
    mine = group * 16 + f
    row = lax.broadcasted_iota(jnp.int32, (16, 128), 0)
    lane = lax.broadcasted_iota(jnp.int32, (16, 128), 1)
    here = lane == row + mine % 8 * 16
    label_weight = jnp.exp(as_column(labels[...].astype(F32)))
    score_row = jnp.sum(jnp.where(here, score, 0.0), axis=0, keepdims=True)
    label_row = jnp.sum(jnp.where(here, label_weight, 0.0), axis=0, keepdims=True)
    table[mine] = jnp.concatenate([score_row, label_row], axis=1)
    scores.start(0)
    slope = inverse * (weight - unit * jnp.mean(weight * unit, axis=1, keepdims=True))
    slope = (slope * (1.0 / TOKENS)).astype(BF)
    pair[:, :D] = slope
    pair[:, D:] = high
    pair_gather.begin()
    everyone[f] = pair[...]
    d_attended = mm(w_out, slope, 1, 1).astype(BF)
    d_att[...] = mm(d_attended, segments(), 1, 0).astype(BF)
    scores.wait()
    scores.start(1)
    attend_back(projected, probs, d_att, d_projected, 0, 8)
    scores.wait()
    scores.start(2)
    pair_gather.near_sides()
    attend_back(projected, probs, d_att, d_projected, 8, 12)
    scores.wait()
    scores.start(3)
    attend_back(projected, probs, d_att, d_projected, 12, 20)
    pair_gather.near_opposite()
    attend_back(projected, probs, d_att, d_projected, 20, 32)
    scores.wait()
    pair_gather.far_sides()
    loss_value, factors = listwise(table, lengths, group)
    loss[...] = loss_value
    own = jnp.where(f // 8 == 0, factors[0], factors[1])
    factor = jnp.sum(jnp.where(here, own, 0.0), axis=1, keepdims=True)
    token = lax.broadcasted_iota(jnp.int32, (PASS, ROWS), 1) // TOKENS
    passage = lax.broadcasted_iota(jnp.int32, (PASS, ROWS), 0)
    factor_row = jnp.sum(jnp.where(token == passage, factor, 0.0), axis=0, keepdims=True)

    @pl.loop(0, 12)
    def _(i):
        at = pl.ds(pl.multiple_of(i * 128, 128), 128)
        d_projected[at, :] = (d_projected[at, :].astype(F32) * factor_row).astype(BF)

    ring = Scatter(blocks, slabs, first, second, third, fourth, (ring_send, ring_recv))
    units = [(step, half) for step in ORDER for half in range(2)]
    swaps = {}

    def unit(step, half):
        if half == 0:
            start = pl.multiple_of((x + step) % 4 * 512, 512)
            rhs = normal[:, pl.ds(start, 512)]
        else:
            at = [pl.multiple_of((i * 4 + (y + step) % 4) * 128, 128) for i in range(4)]
            rhs = jnp.concatenate([normal[:, pl.ds(a, 128)] for a in at], axis=1)
        for parity, target in ((1 - c, leaving), (c, blocks)):
            starts = [pl.multiple_of((4 * half + 2 * i + parity) * 192, 64) for i in range(2)]
            lhs = jnp.concatenate([d_projected[pl.ds(s, 192), :] for s in starts], axis=0)
            out = mm(lhs, rhs, 1, 0).astype(BF)
            for j in range(4):
                target[half, step % 4, j] = out[:, j * 128 : (j + 1) * 128]
        swaps[step, half] = send(
            leaving.at[half, step % 4],
            arriving.at[half, step % 4],
            (core_send, core_recv),
            len(swaps),
            {"c": 1 - c},
        )

    def joined(step, half):
        swaps[step, half].wait_recv()
        at = step % 4
        mine = blocks[half, at].astype(F32)
        blocks[half, at] = (mine + arriving[half, at].astype(F32)).astype(BF)

    for n, (step, half) in enumerate(units):
        unit(step, half)
        if n:
            joined(*units[n - 1])
            if units[n - 1][0] == 2:
                ring.wide_first(units[n - 1][1])
        if n == 5:
            ring.wide_second(0, 1)
        if n == 6:
            ring.wide_second(1, 1)
            ring.wide_second(0, -1)
    joined(*units[-1])
    ring.wide_second(1, -1)

    pair_gather.far_opposite()
    lanes = pl.ds(pl.multiple_of(D + f // 2 * 128, 128), 128)
    group_factor = jnp.concatenate([as_column(factors[0]), as_column(factors[1])], axis=0)
    sums = (everyone[:, :, lanes].reshape(256, 128).astype(F32) * group_factor).astype(BF)
    wide[...] = mm(sums, everyone[:, :, :D].reshape(256, D), 0, 0)
    mine = wide[pl.ds(pl.multiple_of(f % 2 * 64, 64), 64), :].astype(BF)
    for l in range(8):
        outer[l] = mine[:, l * 256 : (l + 1) * 256]
    out_copies = [
        send(outer.at[w["z"] * 2 + w["c"]], outer_in.at[k], (list_send, list_recv), k, w)
        for k, w in enumerate(outers)
    ]
    ring.wide_last(0)
    ring.wide_last(1)
    ring.narrow_second(0)
    ring.narrow_second(1)
    total = outer[z * 2 + c].astype(F32)
    for k, copy in enumerate(out_copies):
        copy.wait()
        total = total + outer_in[k].astype(F32)
    grad_out[...] = total
    for half in range(2):
        both = ring.narrow_last(half).astype(BF)
        layers[2 * half] = both[:192]
        layers[2 * half + 1] = both[192:]
    layer_copies = [
        send(layers.at[(z + j) % 4], layers_in.at[j - 1], (list_send, list_recv), 6 + j, {"z": (z + j) % 4})
        for j in (1, 2, 3)
    ]
    total = layers[z].astype(F32)
    for k, copy in enumerate(layer_copies):
        copy.wait()
        total = total + layers_in[k].astype(F32)
    grad_qkv[...] = total.T
    qkv_gather.end()
    out_gather.end()
    pair_gather.end()
    ring.end()
    for copy in swaps.values():
        copy.wait_send()


def vm():
    return pl.BlockSpec(memory_space=pltpu.VMEM)


def shape(*dims, dtype=BF):
    return jax.ShapeDtypeStruct(dims, dtype)


def semaphores(count):
    return [pltpu.SemaphoreType.DMA((count,))] * 2


def local(hidden, norm_gain, w_qkv, w_out, final_gain, w_score, prior, labels, lengths):
    loss, grad_qkv, grad_out = pl.pallas_call(
        whole_body,
        out_shape=(
            shape(1, 1, dtype=F32),
            shape(128, 192, dtype=F32),
            shape(64, 256, dtype=F32),
        ),
        in_specs=[vm()] * 9,
        out_specs=(vm(),) * 3,
        scratch_shapes=[
            pltpu.VMEM((ROWS, D), BF),
            pltpu.VMEM((PASS, D), F32),
            pltpu.VMEM((16, COLS, 128), BF),
            pltpu.VMEM((COLS, ROWS), F32),
            pltpu.VMEM((COLS, ROWS), BF),
            pltpu.VMEM((32, 64, 512), BF),
            pltpu.VMEM((QW, ROWS), BF),
            pltpu.VMEM((16, 64, D), BF),
            pltpu.VMEM((128, 1, 256), F32),
            pltpu.VMEM((PASS, D + QW), BF),
            pltpu.VMEM((COLS, ROWS), BF),
            pltpu.VMEM((16, PASS, D + QW), BF),
            pltpu.VMEM((128, D), F32),
            pltpu.VMEM((8, 64, 256), BF),
            pltpu.VMEM((7, 64, 256), BF),
            pltpu.VMEM((2, 4, 4, 384, 128), BF),
            pltpu.VMEM((2, 4, 4, 384, 128), BF),
            pltpu.VMEM((2, 4, 4, 384, 128), BF),
            pltpu.VMEM((2, 4, 384, 128), BF),
            pltpu.VMEM((2, 2, 4, 192, 128), BF),
            pltpu.VMEM((2, 2, 4, 384, 128), BF),
            pltpu.VMEM((2, 2, 192, 128), BF),
            pltpu.VMEM((2, 2, 384, 128), BF),
            pltpu.VMEM((4, 192, 128), BF),
            pltpu.VMEM((3, 192, 128), BF),
        ]
        + semaphores(70)
        + semaphores(70)
        + semaphores(10)
        + semaphores(40)
        + semaphores(8)
        + semaphores(16)
        + semaphores(10),
        compiler_params=pltpu.CompilerParams(
            vmem_limit_bytes=VMEM_CAP, has_side_effects=True, collective_id=0
        ),
        name="whole",
    )(
        hidden.reshape(ROWS, D), norm_gain.reshape(1, D), w_qkv, w_out,
        final_gain.reshape(1, D), w_score.reshape(1, D),
        prior.reshape(1, PASS), labels.reshape(1, PASS), lengths.reshape(1, -1),
    )
    return loss.reshape(()), grad_qkv, grad_out


def solution(mesh):
    torus = Mesh(mesh.devices.reshape(4, 2, 4, 4), ALL)
    in_specs = (
        P(ALL, None, None), P(), P(FSDP, None), P(FSDP, None), P(), P(), P(ALL), P(ALL), P(),
    )
    out_specs = (P(), P(FSDP, LIST), P(FSDP, LIST))
    return jax.shard_map(local, mesh=torus, in_specs=in_specs, out_specs=out_specs, check_vma=False)
```

```python
import jax
import jax.numpy as jnp
from jax import lax
from jax.experimental import pallas as pl
from jax.experimental.pallas import tpu as pltpu
from jax.sharding import Mesh
from jax.sharding import PartitionSpec as P

BF = jnp.bfloat16
F32 = jnp.float32
FSDP = ("x", "y")
LIST = ("z", "c")
ALL = ("z", "c", "x", "y")
EPS = 1e-05
SCALE = 64.0
TOKENS = 64
PASS = 16
ROWS = PASS * TOKENS
D = 2048
COLS = 1536
QW = 1024
KVW = 256
VMEM_CAP = 63 * 1024 * 1024


def mm(a, b, ca, cb):
    return lax.dot_general(a, b, (((ca,), (cb,)), ((), ())), preferred_element_type=F32)


def norm_rows(hidden, gain, normal, hsum):
    g = gain[...]

    @pl.loop(0, PASS)
    def _(p):
        at = pl.ds(pl.multiple_of(p * TOKENS, TOKENS), TOKENS)
        x = hidden[at, :].astype(F32)
        mean_square = jnp.mean(x * x, axis=1, keepdims=True)
        normal[at, :] = (x * lax.rsqrt(mean_square + EPS) * g).astype(BF)
        hsum[pl.ds(p, 1), :] = jnp.sum(x, axis=0, keepdims=True)


SIDES = (1, -1)


class Gather:
    def __init__(self, view, own, sems, across):
        self.view, self.own, self.sems, self.across = view, own, sems, across
        self.z, self.c, self.x, self.y = place()
        self.copies = {}

    def slot(self, half, near, far):
        dx, dy = (far, near) if half == 0 else (near, far)
        return (self.x + dx) % 4 * 4 + (self.y + dy) % 4

    def peer(self, half, stage, step):
        name = "yx"[(half + stage) % 2]
        return {name: ((self.y if name == "y" else self.x) + step) % 4}

    def go(self, key, src, dst, where):
        self.copies[key] = send(src, dst, self.sems, len(self.copies), where)

    def pass_on(self, half, near, far):
        slot = self.slot(half, near, far)
        if far == 0:
            for step in SIDES:
                ref = self.view(slot, half, None)
                self.go((half, 2, near, step), ref, ref, self.peer(half, 1, step))
        if self.across:
            ref = self.view(slot, half, None)
            self.go((half, 5, near, far), ref, ref, {"c": 1 - self.c})

    def relay(self, key, half, stage, slot, step):
        ref = self.view(slot, half, 0 if step == 1 else 1)
        self.go(key, ref, ref, self.peer(half, stage, step))

    def begin(self):
        for half in range(2):
            for stage, key in ((0, (half, 1)), (1, (half, 2, 0))):
                for step in SIDES:
                    self.go(
                        (*key, step),
                        self.own(half),
                        self.view(self.slot(half, 0, 0), half, None),
                        self.peer(half, stage, step),
                    )

    def near_sides(self):
        for half in range(2):
            for step in SIDES:
                self.copies[half, 1, step].wait_recv()
                self.relay((half, 3, step), half, 0, self.slot(half, -step, 0), step)
                self.pass_on(half, -step, 0)

    def near_opposite(self):
        for half in range(2):
            for step in SIDES:
                self.copies[half, 3, step].wait_recv()
            self.pass_on(half, 2, 0)

    def far_sides(self):
        for near in (0, 1, -1, 2):
            for half in range(2):
                for step in SIDES:
                    self.copies[half, 2, near, step].wait_recv()
                    slot = self.slot(half, near, -step)
                    self.relay((half, 4, near, step), half, 1, slot, step)
                    self.pass_on(half, near, -step)

    def far_opposite(self):
        for near in (0, 1, -1, 2):
            for half in range(2):
                for step in SIDES:
                    self.copies[half, 4, near, step].wait_recv()
                self.pass_on(half, near, 2)

    def across_sides(self):
        self.across_wait(lambda near, far: near != 2 and far != 2)

    def across_rest(self):
        self.across_wait(lambda near, far: near == 2 or far == 2)

    def across_wait(self, chosen):
        for key, copy in self.copies.items():
            if key[1] == 5 and chosen(key[2], key[3]):
                copy.wait_recv()

    def end(self):
        for copy in self.copies.values():
            copy.wait_send()


def plane_peers(x, y, c):
    return [{"x": (x + 1) % 4}, {"x": (x + 3) % 4}, {"y": (y + 1) % 4}, {"y": (y + 3) % 4}, {"c": 1 - c}]


def project_part(wt, normal, total, projected, slots, last, begin, end):
    @pl.loop(begin, end)
    def _(n):
        at = pl.multiple_of(n * 256, 256)
        cols = [pl.ds(pl.multiple_of(s * 128, 128), 128) for s in slots]
        rhs = jnp.concatenate([normal[pl.ds(at, 256), col] for col in cols], axis=1)
        for m in range(2):
            rows = pl.ds(m * 768, 768)
            lhs = jnp.concatenate([wt[s, rows, :] for s in slots], axis=1)
            out = mm(lhs, rhs, 1, 1)
            if last:
                projected[rows, pl.ds(at, 256)] = (total[rows, pl.ds(at, 256)] + out).astype(BF)
            else:
                total[rows, pl.ds(at, 256)] = out


def halves_mask():
    return lax.broadcasted_iota(jnp.int32, (1, 512), 1) % 128 < 64


def side_by_side(block):
    return jnp.concatenate([block[r * 64 : (r + 1) * 64] for r in range(4)], axis=1)


def own_blocks(full, first):
    return jnp.where(first, full[:64], full[64:])


def both_blocks(part, first):
    zero = jnp.zeros_like(part)
    return jnp.concatenate([jnp.where(first, part, zero), jnp.where(first, zero, part)], axis=0)


def places(i):
    g, pair = i // 8, i % 8
    lanes = pl.ds(pl.multiple_of(pair * 128, 128), 128)
    q_rows = pl.ds(pl.multiple_of(g * 256, 256), 256)
    k_rows = pl.ds(pl.multiple_of(QW + g * 64, 64), 64)
    v_rows = pl.ds(pl.multiple_of(QW + KVW + g * 64, 64), 64)
    return g, lanes, q_rows, k_rows, v_rows


def segments():
    row = lax.broadcasted_iota(jnp.int32, (PASS, ROWS), 0)
    lane = lax.broadcasted_iota(jnp.int32, (PASS, ROWS), 1)
    return (lane // TOKENS == row).astype(F32).astype(BF)


UNROLL = 4


def attend(projected, probs, attended, begin, end):
    @pl.loop(begin // UNROLL, end // UNROLL)
    def _(t):
        first = halves_mask()
        ids = [t * UNROLL + u for u in range(UNROLL)]
        spots = [places(i) for i in ids]
        queries = [side_by_side(projected[s[2], s[1]]) for s in spots]
        keys = [projected[s[3], s[1]] for s in spots]
        values = [projected[s[4], s[1]] for s in spots]
        parts = []
        for full in [mm(k, q, 0, 0) for k, q in zip(keys, queries)]:
            scores = own_blocks(full, first) * 0.125
            expo = jnp.exp(scores - jnp.max(scores, axis=0, keepdims=True))
            parts.append((expo * (1.0 / jnp.sum(expo, axis=0, keepdims=True))).astype(BF))
        outs = [mm(v, both_blocks(part, first), 1, 0).astype(BF) for v, part in zip(values, parts)]
        for i, spot, part, out in zip(ids, spots, parts, outs):
            probs[i] = part
            for r in range(4):
                rows = pl.ds(pl.multiple_of(spot[0] * 256 + r * 64, 64), 64)
                attended[rows, spot[1]] = out[:, r * 128 : (r + 1) * 128]


def attend_back(projected, probs, d_att, d_projected, begin, end):
    @pl.loop(begin // UNROLL, end // UNROLL)
    def _(t):
        first = halves_mask()
        ids = [t * UNROLL + u for u in range(UNROLL)]
        spots = [places(i) for i in ids]
        queries = [side_by_side(projected[s[2], s[1]]) for s in spots]
        outs = [side_by_side(d_att[s[2], s[1]]) for s in spots]
        keys = [projected[s[3], s[1]] for s in spots]
        values = [projected[s[4], s[1]] for s in spots]
        parts = [probs[i] for i in ids]
        d_full = [mm(v, da, 0, 0) for v, da in zip(values, outs)]
        dv = [mm(da, both_blocks(part, first), 1, 1).astype(BF) for da, part in zip(outs, parts)]
        d_scores = []
        for full, part in zip(d_full, parts):
            d_probs, wide = own_blocks(full, first), part.astype(F32)
            inner = jnp.sum(wide * d_probs, axis=0, keepdims=True)
            d_scores.append(both_blocks((wide * (d_probs - inner) * 0.125).astype(BF), first))
        dq = [mm(k, ds, 1, 0).astype(BF) for k, ds in zip(keys, d_scores)]
        dk = [mm(q, ds, 1, 1).astype(BF) for q, ds in zip(queries, d_scores)]
        for u, spot in enumerate(spots):
            for r in range(4):
                rows = pl.ds(pl.multiple_of(spot[0] * 256 + r * 64, 64), 64)
                d_projected[rows, spot[1]] = dq[u][:, r * 128 : (r + 1) * 128]
            d_projected[spot[3], spot[1]] = dk[u]
            d_projected[spot[4], spot[1]] = dv[u]


def send(src, dst, sems, slot, where):
    copy = pltpu.make_async_remote_copy(
        src_ref=src,
        dst_ref=dst,
        send_sem=sems[0].at[slot],
        recv_sem=sems[1].at[slot],
        device_id=where,
        device_id_type=pl.DeviceIdType.MESH,
    )
    copy.start()
    return copy


def place():
    return tuple(lax.axis_index(a) for a in ALL)


def greet(peers):
    barrier = pltpu.get_barrier_semaphore()
    for where in peers:
        pl.semaphore_signal(barrier, inc=1, device_id=where, device_id_type=pl.DeviceIdType.MESH)
    pl.semaphore_wait(barrier, len(peers))


def axis_peers(name, at):
    return [{name: (at + j) % 4} for j in (1, 2, 3)]


class Exchange:
    def __init__(self, table, sems):
        z, c, x, y = place()
        group = z * 2 + c
        mine = (group * 4 + x) * 4 + y
        self.table, self.sems, self.used, self.copies = table, sems, 0, []
        self.stages = [
            (axis_peers("y", y), mine, 1),
            (axis_peers("x", x), mine - y, 4),
            ([{"c": 1 - c}], group * 16, 16),
            (axis_peers("z", z), z * 32, 32),
        ]

    def start(self, stage):
        peers, start, size = self.stages[stage]
        block = self.table.at[pl.ds(start, size)]
        self.copies = [send(block, block, self.sems, self.used + j, w) for j, w in enumerate(peers)]
        self.used += len(peers)

    def wait(self):
        for copy in self.copies:
            copy.wait()


def listwise(table, lengths, group):
    length_row = lengths[...].astype(F32)
    row = lax.broadcasted_iota(jnp.int32, (64, 64), 0)
    lane = lax.broadcasted_iota(jnp.int32, (64, 64), 1)
    ends = jnp.sum(jnp.where(lane <= row, length_row, 0.0), axis=1, keepdims=True)
    starts = jnp.sum(jnp.where(lane < row, length_row, 0.0), axis=1, keepdims=True)
    lanes = lax.broadcasted_iota(jnp.int32, (1, 128), 1).astype(F32)
    score, weight, member = [], [], []
    top = jnp.full((64, 128), -1e30, F32)
    labels = jnp.zeros((64, 128), F32)
    for r in range(16):
        both = table[8 * r]
        for j in range(1, 8):
            both = both + table[8 * r + j]
        score.append(both[:, :128])
        weight.append(both[:, 128:])
        position = lanes + 128.0 * r
        member.append(jnp.logical_and(position >= starts, position < ends))
        top = jnp.maximum(top, jnp.where(member[r], score[r], -1e30))
        labels = labels + jnp.where(member[r], weight[r], 0.0)
    peak = jnp.max(top, axis=1, keepdims=True)
    label_total = jnp.sum(labels, axis=1, keepdims=True)
    total = jnp.zeros((64, 128), F32)
    for r in range(16):
        total = total + jnp.exp(jnp.where(member[r], score[r] - peak, -1e30))
    log_norm = peak + jnp.log(jnp.sum(total, axis=1, keepdims=True))
    terms = jnp.zeros((1, 128), F32)
    own = [jnp.zeros((1, 128), F32)] * 2
    for r in range(16):
        norm = jnp.sum(jnp.where(member[r], log_norm, 0.0), axis=0, keepdims=True)
        labels = jnp.sum(jnp.where(member[r], label_total, 0.0), axis=0, keepdims=True)
        log_prob = score[r] - norm
        target = weight[r] / labels
        terms = terms + target * log_prob
        d_score = SCALE * (jnp.exp(log_prob) - target)
        own[r % 2] = own[r % 2] + jnp.where(group == r // 2, d_score, 0.0)
    return -SCALE * jnp.sum(terms, axis=1, keepdims=True), own


ORDER = (2, 1, -1, 0)


class Scatter:
    def __init__(self, blocks, slabs, first, second, third, fourth, sems):
        self.blocks, self.slabs, self.sems = blocks, slabs, sems
        self.first, self.second, self.third, self.fourth = first, second, third, fourth
        self.z, self.c, self.x, self.y = place()
        self.copies = {}

    def at(self, half, stage):
        return self.x if (half + stage) % 2 == 0 else self.y

    def go(self, key, src, dst, half, stage, step):
        name = "xy"[(half + stage) % 2]
        where = {name: (self.at(half, stage) + step) % 4}
        self.copies[key] = send(src, dst, self.sems, len(self.copies), where)

    def part(self, step):
        return pl.ds(0 if step == 1 else 192, 192)

    def wide_first(self, half):
        block = self.blocks.at[half, 2]
        for k, step in enumerate(SIDES):
            self.go((half, 1, step), block.at[:, self.part(step), :], self.first.at[half, k], half, 0, step)

    def rest(self, step):
        return pl.ds(192 if step == 1 else 0, 192)

    def wide_early(self, half, step):
        k, rows = SIDES.index(step), self.rest(step)
        src, dst = self.blocks.at[half, step % 4, :, rows, :], self.second.at[half, k, :, rows, :]
        self.go((half, 2, step), src, dst, half, 0, step)

    def wide_late(self, half, step):
        k, rows, at = SIDES.index(step), self.part(step), step % 4
        self.copies[half, 1, step].wait_recv()
        for b in ORDER:
            slot = (self.at(half, 1) + b) % 4
            mine = self.blocks[half, at, slot, rows, :].astype(F32)
            self.blocks[half, at, slot, rows, :] = (
                mine + self.first[half, k, slot].astype(F32)
            ).astype(BF)
            src, dst = self.blocks.at[half, at, slot, rows, :], self.second.at[half, k, slot, rows, :]
            self.go((half, 2, step, b), src, dst, half, 0, step)

    def wide_last(self):
        for b in ORDER:
            for half in range(2):
                slot = (self.at(half, 1) + b) % 4
                total = self.blocks[half, 0, slot].astype(F32)
                for k, step in enumerate(SIDES):
                    if b == 2:
                        self.copies[half, 2, step].wait_recv()
                    self.copies[half, 2, step, b].wait_recv()
                    total = total + self.second[half, k, slot].astype(F32)
                self.slabs[half, slot] = total.astype(BF)
                slab = self.slabs.at[half, slot]
                if b == 2:
                    for k, step in enumerate(SIDES):
                        src = slab.at[self.part(step), :]
                        self.go((half, 3, step), src, self.third.at[half, k], half, 1, step)
                elif b:
                    k, rows = SIDES.index(b), self.rest(b)
                    dst = self.fourth.at[half, k, rows, :]
                    self.go((half, 4, b), slab.at[rows, :], dst, half, 1, b)

    def narrow_late(self, half):
        for k, step in enumerate(SIDES):
            self.copies[half, 3, step].wait_recv()
            rows = self.part(step)
            at = (self.at(half, 1) + step) % 4
            mine = self.slabs[half, at, rows, :].astype(F32)
            self.slabs[half, at, rows, :] = (mine + self.third[half, k].astype(F32)).astype(BF)
            src, dst = self.slabs.at[half, at, rows, :], self.fourth.at[half, k, rows, :]
            self.go((half, 5, step), src, dst, half, 1, step)

    def narrow_last(self, half):
        total = self.slabs[half, self.at(half, 1)].astype(F32)
        for k, step in enumerate(SIDES):
            self.copies[half, 4, step].wait_recv()
            self.copies[half, 5, step].wait_recv()
            total = total + self.fourth[half, k].astype(F32)
        return total

    def end(self):
        for copy in self.copies.values():
            copy.wait_send()


def outer_peers(z, c):
    return [
        {"z": (z + j) % 4, "c": (c + k) % 2} for j in range(4) for k in range(2) if (j, k) != (0, 0)
    ]


def as_column(row):
    count = row.shape[1]
    same = lax.broadcasted_iota(jnp.int32, (count, count), 0) == lax.broadcasted_iota(
        jnp.int32, (count, count), 1
    )
    return jnp.sum(jnp.where(same, row, 0.0), axis=1, keepdims=True)


def whole_body(
    hidden, gain, w_qkv, w_out_own, final_gain, w_score, prior, labels, lengths,
    loss, grad_qkv, grad_out,
    normal, hsum, wt, total_f, projected, probs, attended, w_blocks, table, pair,
    d_projected, everyone, wide, outer, outer_in,
    leaving, arriving, blocks, slabs, first, second, third, fourth, layers, layers_in,
    qkv_send, qkv_recv, out_send, out_recv, table_send, table_recv,
    pair_send, pair_recv, core_send, core_recv, ring_send, ring_recv, list_send, list_recv,
):
    z, c, x, y = place()
    d_att = attended
    f = x * 4 + y
    group = z * 2 + c

    def qkv_rows(half, part, core):
        start, size = half * 384, 384
        if part is not None:
            start, size = start + part * 192, 192
        return pl.ds(pl.multiple_of(core * 768 + start, 64), size)

    def out_rows(half):
        return pl.ds(pl.multiple_of(c * 32 + half * 16, 16), 16)

    def out_cols(part):
        return pl.ds(0, D) if part is None else pl.ds(part * 1024, 1024)

    def pair_cols(half, part):
        return pl.ds(half * 1536, 1536) if part is None else pl.ds(half * 1536 + part * 768, 768)

    qkv_gather = Gather(
        lambda slot, half, part: wt.at[slot, qkv_rows(half, part, c), :],
        lambda half: wt.at[f, qkv_rows(half, None, c), :],
        (qkv_send, qkv_recv),
        True,
    )
    out_gather = Gather(
        lambda slot, half, part: w_blocks.at[slot, out_rows(half), out_cols(part)],
        lambda half: w_out_own.at[out_rows(half), :],
        (out_send, out_recv),
        True,
    )
    pair_gather = Gather(
        lambda slot, half, part: everyone.at[slot, :, pair_cols(half, part)],
        lambda half: pair.at[:, pair_cols(half, None)],
        (pair_send, pair_recv),
        False,
    )
    scores = Exchange(table, (table_send, table_recv))
    outers = outer_peers(z, c)

    def turned(core):
        for half in range(2):
            cols = pl.ds(pl.multiple_of(core * 768 + half * 384, 128), 384)
            wt[f, qkv_rows(half, None, core), :] = w_qkv[:, cols].T

    turned(c)
    greet(axis_peers("y", y) + axis_peers("x", x) + outers)
    qkv_gather.begin()
    turned(1 - c)
    w_blocks[f] = w_out_own[...]
    norm_rows(hidden, gain, normal, hsum)
    qkv_gather.near_sides()
    qkv_gather.near_opposite()
    out_gather.begin()
    qkv_gather.far_sides()
    out_gather.near_sides()
    qkv_gather.across_sides()
    steps = [(0, 0), (0, 1), (0, -1), (1, 0), (-1, 0), (1, 1), (1, -1), (-1, 1)]
    early = [(x + i) % 4 * 4 + (y + j) % 4 for i, j in steps]
    every = [(i, j) for i in (0, 1, 2, -1) for j in (0, 1, 2, -1)]
    late = [(x + i) % 4 * 4 + (y + j) % 4 for i, j in every if (i, j) not in steps]
    project_part(wt, normal, total_f, projected, early, False, 0, 4)
    qkv_gather.far_opposite()
    out_gather.near_opposite()
    qkv_gather.across_rest()
    project_part(wt, normal, total_f, projected, late, True, 0, 2)
    out_gather.far_sides()
    project_part(wt, normal, total_f, projected, late, True, 2, 4)
    attend(projected, probs, attended, 0, 16)
    out_gather.far_opposite()
    attend(projected, probs, attended, 16, 32)
    out_gather.across_sides()
    out_gather.across_rest()

    w_out = w_blocks[...].reshape(QW, D)
    sums = mm(segments(), attended[...], 1, 1)
    high = sums.astype(BF)
    low = (sums - high.astype(F32)).astype(BF)
    mixed = mm(jnp.concatenate([high, low], axis=0), w_out, 1, 0)
    pooled = (hsum[...] + mixed[:16] + mixed[16:]) * (1.0 / TOKENS)
    inverse = lax.rsqrt(jnp.mean(pooled * pooled, axis=1, keepdims=True) + EPS)
    unit = pooled * inverse
    weight = final_gain[...] * w_score[...]
    score = jnp.sum(unit * weight, axis=1, keepdims=True) + as_column(prior[...])
    mine = group * 16 + f
    row = lax.broadcasted_iota(jnp.int32, (16, 128), 0)
    lane = lax.broadcasted_iota(jnp.int32, (16, 128), 1)
    here = lane == row + mine % 8 * 16
    label_weight = jnp.exp(as_column(labels[...].astype(F32)))
    score_row = jnp.sum(jnp.where(here, score, 0.0), axis=0, keepdims=True)
    label_row = jnp.sum(jnp.where(here, label_weight, 0.0), axis=0, keepdims=True)
    table[mine] = jnp.concatenate([score_row, label_row], axis=1)
    scores.start(0)
    slope = inverse * (weight - unit * jnp.mean(weight * unit, axis=1, keepdims=True))
    slope = (slope * (1.0 / TOKENS)).astype(BF)
    pair[:, :D] = slope
    pair[:, D:] = high
    pair_gather.begin()
    everyone[f] = pair[...]
    d_attended = mm(w_out, slope, 1, 1).astype(BF)
    d_att[...] = mm(d_attended, segments(), 1, 0).astype(BF)
    scores.wait()
    scores.start(1)
    attend_back(projected, probs, d_att, d_projected, 0, 8)
    scores.wait()
    scores.start(2)
    pair_gather.near_sides()
    attend_back(projected, probs, d_att, d_projected, 8, 12)
    scores.wait()
    scores.start(3)
    attend_back(projected, probs, d_att, d_projected, 12, 20)
    pair_gather.near_opposite()
    attend_back(projected, probs, d_att, d_projected, 20, 32)
    scores.wait()
    pair_gather.far_sides()
    loss_value, factors = listwise(table, lengths, group)
    loss[...] = loss_value
    own = jnp.where(f // 8 == 0, factors[0], factors[1])
    factor = jnp.sum(jnp.where(here, own, 0.0), axis=1, keepdims=True)
    token = lax.broadcasted_iota(jnp.int32, (PASS, ROWS), 1) // TOKENS
    passage = lax.broadcasted_iota(jnp.int32, (PASS, ROWS), 0)
    factor_row = jnp.sum(jnp.where(token == passage, factor, 0.0), axis=0, keepdims=True)

    @pl.loop(0, 12)
    def _(i):
        at = pl.ds(pl.multiple_of(i * 128, 128), 128)
        d_projected[at, :] = (d_projected[at, :].astype(F32) * factor_row).astype(BF)

    ring = Scatter(blocks, slabs, first, second, third, fourth, (ring_send, ring_recv))
    units = [(step, half) for step in ORDER for half in range(2)]
    swaps = {}

    def unit(step, half):
        if half == 0:
            start = pl.multiple_of((x + step) % 4 * 512, 512)
            rhs = normal[:, pl.ds(start, 512)]
        else:
            at = [pl.multiple_of((i * 4 + (y + step) % 4) * 128, 128) for i in range(4)]
            rhs = jnp.concatenate([normal[:, pl.ds(a, 128)] for a in at], axis=1)
        for parity, target in ((1 - c, leaving), (c, blocks)):
            starts = [pl.multiple_of((4 * half + 2 * i + parity) * 192, 64) for i in range(2)]
            lhs = jnp.concatenate([d_projected[pl.ds(s, 192), :] for s in starts], axis=0)
            out = mm(lhs, rhs, 1, 0).astype(BF)
            for j in range(4):
                target[half, step % 4, j] = out[:, j * 128 : (j + 1) * 128]
        swaps[step, half] = send(
            leaving.at[half, step % 4],
            arriving.at[half, step % 4],
            (core_send, core_recv),
            len(swaps),
            {"c": 1 - c},
        )

    def joined(step, half):
        swaps[step, half].wait_recv()
        at = step % 4
        mine = blocks[half, at].astype(F32)
        blocks[half, at] = (mine + arriving[half, at].astype(F32)).astype(BF)

    def passed(step, half):
        joined(step, half)
        if step == 2:
            ring.wide_first(half)
        elif step:
            ring.wide_early(half, step)

    for n, (step, half) in enumerate(units):
        unit(step, half)
        if n:
            passed(*units[n - 1])
    passed(*units[-1])
    for half in range(2):
        for step in SIDES:
            ring.wide_late(half, step)

    pair_gather.far_opposite()
    lanes = pl.ds(pl.multiple_of(D + f // 2 * 128, 128), 128)
    group_factor = jnp.concatenate([as_column(factors[0]), as_column(factors[1])], axis=0)
    sums = (everyone[:, :, lanes].reshape(256, 128).astype(F32) * group_factor).astype(BF)
    wide[...] = mm(sums, everyone[:, :, :D].reshape(256, D), 0, 0)
    mine = wide[pl.ds(pl.multiple_of(f % 2 * 64, 64), 64), :].astype(BF)
    for l in range(8):
        outer[l] = mine[:, l * 256 : (l + 1) * 256]
    out_copies = [
        send(outer.at[w["z"] * 2 + w["c"]], outer_in.at[k], (list_send, list_recv), k, w)
        for k, w in enumerate(outers)
    ]
    ring.wide_last()
    ring.narrow_late(0)
    ring.narrow_late(1)
    total = outer[z * 2 + c].astype(F32)
    for k, copy in enumerate(out_copies):
        copy.wait()
        total = total + outer_in[k].astype(F32)
    grad_out[...] = total
    for half in range(2):
        both = ring.narrow_last(half).astype(BF)
        layers[2 * half] = both[:192]
        layers[2 * half + 1] = both[192:]
    layer_copies = [
        send(layers.at[(z + j) % 4], layers_in.at[j - 1], (list_send, list_recv), 6 + j, {"z": (z + j) % 4})
        for j in (1, 2, 3)
    ]
    total = layers[z].astype(F32)
    for k, copy in enumerate(layer_copies):
        copy.wait()
        total = total + layers_in[k].astype(F32)
    grad_qkv[...] = total.T
    qkv_gather.end()
    out_gather.end()
    pair_gather.end()
    ring.end()
    for copy in swaps.values():
        copy.wait_send()


def vm():
    return pl.BlockSpec(memory_space=pltpu.VMEM)


def shape(*dims, dtype=BF):
    return jax.ShapeDtypeStruct(dims, dtype)


def semaphores(count):
    return [pltpu.SemaphoreType.DMA((count,))] * 2


def local(hidden, norm_gain, w_qkv, w_out, final_gain, w_score, prior, labels, lengths):
    loss, grad_qkv, grad_out = pl.pallas_call(
        whole_body,
        out_shape=(
            shape(1, 1, dtype=F32),
            shape(128, 192, dtype=F32),
            shape(64, 256, dtype=F32),
        ),
        in_specs=[vm()] * 9,
        out_specs=(vm(),) * 3,
        scratch_shapes=[
            pltpu.VMEM((ROWS, D), BF),
            pltpu.VMEM((PASS, D), F32),
            pltpu.VMEM((16, COLS, 128), BF),
            pltpu.VMEM((COLS, ROWS), F32),
            pltpu.VMEM((COLS, ROWS), BF),
            pltpu.VMEM((32, 64, 512), BF),
            pltpu.VMEM((QW, ROWS), BF),
            pltpu.VMEM((16, 64, D), BF),
            pltpu.VMEM((128, 1, 256), F32),
            pltpu.VMEM((PASS, D + QW), BF),
            pltpu.VMEM((COLS, ROWS), BF),
            pltpu.VMEM((16, PASS, D + QW), BF),
            pltpu.VMEM((128, D), F32),
            pltpu.VMEM((8, 64, 256), BF),
            pltpu.VMEM((7, 64, 256), BF),
            pltpu.VMEM((2, 4, 4, 384, 128), BF),
            pltpu.VMEM((2, 4, 4, 384, 128), BF),
            pltpu.VMEM((2, 4, 4, 384, 128), BF),
            pltpu.VMEM((2, 4, 384, 128), BF),
            pltpu.VMEM((2, 2, 4, 192, 128), BF),
            pltpu.VMEM((2, 2, 4, 384, 128), BF),
            pltpu.VMEM((2, 2, 192, 128), BF),
            pltpu.VMEM((2, 2, 384, 128), BF),
            pltpu.VMEM((4, 192, 128), BF),
            pltpu.VMEM((3, 192, 128), BF),
        ]
        + semaphores(70)
        + semaphores(70)
        + semaphores(10)
        + semaphores(40)
        + semaphores(8)
        + semaphores(36)
        + semaphores(10),
        compiler_params=pltpu.CompilerParams(
            vmem_limit_bytes=VMEM_CAP, has_side_effects=True, collective_id=0
        ),
        name="whole",
    )(
        hidden.reshape(ROWS, D), norm_gain.reshape(1, D), w_qkv, w_out,
        final_gain.reshape(1, D), w_score.reshape(1, D),
        prior.reshape(1, PASS), labels.reshape(1, PASS), lengths.reshape(1, -1),
    )
    return loss.reshape(()), grad_qkv, grad_out


def solution(mesh):
    torus = Mesh(mesh.devices.reshape(4, 2, 4, 4), ALL)
    in_specs = (
        P(ALL, None, None), P(), P(FSDP, None), P(FSDP, None), P(), P(), P(ALL), P(ALL), P(),
    )
    out_specs = (P(), P(FSDP, LIST), P(FSDP, LIST))
    return jax.shard_map(local, mesh=torus, in_specs=in_specs, out_specs=out_specs, check_vma=False)
```

```python
import jax
import jax.numpy as jnp
from jax import lax
from jax.experimental import pallas as pl
from jax.experimental.pallas import tpu as pltpu
from jax.sharding import Mesh
from jax.sharding import PartitionSpec as P

BF = jnp.bfloat16
F32 = jnp.float32
FSDP = ("x", "y")
LIST = ("z", "c")
ALL = ("z", "c", "x", "y")
EPS = 1e-05
SCALE = 64.0
TOKENS = 64
PASS = 16
ROWS = PASS * TOKENS
D = 2048
COLS = 1536
QW = 1024
KVW = 256
VMEM_CAP = 63 * 1024 * 1024


def mm(a, b, ca, cb):
    return lax.dot_general(a, b, (((ca,), (cb,)), ((), ())), preferred_element_type=F32)


def norm_rows(hidden, gain, normal, hsum):
    g = gain[...]

    @pl.loop(0, PASS)
    def _(p):
        at = pl.ds(pl.multiple_of(p * TOKENS, TOKENS), TOKENS)
        x = hidden[at, :].astype(F32)
        mean_square = jnp.mean(x * x, axis=1, keepdims=True)
        normal[at, :] = (x * lax.rsqrt(mean_square + EPS) * g).astype(BF)
        hsum[pl.ds(p, 1), :] = jnp.sum(x, axis=0, keepdims=True)


SIDES = (1, -1)


class Gather:
    def __init__(self, view, own, sems, across):
        self.view, self.own, self.sems, self.across = view, own, sems, across
        self.z, self.c, self.x, self.y = place()
        self.copies = {}

    def slot(self, half, near, far):
        dx, dy = (far, near) if half == 0 else (near, far)
        return (self.x + dx) % 4 * 4 + (self.y + dy) % 4

    def peer(self, half, stage, step):
        name = "yx"[(half + stage) % 2]
        return {name: ((self.y if name == "y" else self.x) + step) % 4}

    def go(self, key, src, dst, where):
        self.copies[key] = send(src, dst, self.sems, len(self.copies), where)

    def pass_on(self, half, near, far):
        slot = self.slot(half, near, far)
        if far == 0:
            for step in SIDES:
                ref = self.view(slot, half, None)
                self.go((half, 2, near, step), ref, ref, self.peer(half, 1, step))
        if self.across:
            ref = self.view(slot, half, None)
            self.go((half, 5, near, far), ref, ref, {"c": 1 - self.c})

    def relay(self, key, half, stage, slot, step):
        ref = self.view(slot, half, 0 if step == 1 else 1)
        self.go(key, ref, ref, self.peer(half, stage, step))

    def begin(self):
        for half in range(2):
            for stage, key in ((0, (half, 1)), (1, (half, 2, 0))):
                for step in SIDES:
                    self.go(
                        (*key, step),
                        self.own(half),
                        self.view(self.slot(half, 0, 0), half, None),
                        self.peer(half, stage, step),
                    )

    def near_sides(self):
        for half in range(2):
            for step in SIDES:
                self.copies[half, 1, step].wait_recv()
                self.relay((half, 3, step), half, 0, self.slot(half, -step, 0), step)
                self.pass_on(half, -step, 0)

    def near_opposite(self):
        for half in range(2):
            for step in SIDES:
                self.copies[half, 3, step].wait_recv()
            self.pass_on(half, 2, 0)

    def far_sides(self):
        for near in (0, 1, -1, 2):
            for half in range(2):
                for step in SIDES:
                    self.copies[half, 2, near, step].wait_recv()
                    slot = self.slot(half, near, -step)
                    self.relay((half, 4, near, step), half, 1, slot, step)
                    self.pass_on(half, near, -step)

    def far_opposite(self):
        for near in (0, 1, -1, 2):
            for half in range(2):
                for step in SIDES:
                    self.copies[half, 4, near, step].wait_recv()
                self.pass_on(half, near, 2)

    def across_sides(self):
        self.across_wait(lambda near, far: near != 2 and far != 2)

    def across_rest(self):
        self.across_wait(lambda near, far: near == 2 or far == 2)

    def across_wait(self, chosen):
        for key, copy in self.copies.items():
            if key[1] == 5 and chosen(key[2], key[3]):
                copy.wait_recv()

    def end(self):
        for copy in self.copies.values():
            copy.wait_send()


def plane_peers(x, y, c):
    return [{"x": (x + 1) % 4}, {"x": (x + 3) % 4}, {"y": (y + 1) % 4}, {"y": (y + 3) % 4}, {"c": 1 - c}]


def project_part(wt, normal, total, projected, slots, last, begin, end):
    @pl.loop(begin, end)
    def _(n):
        at = pl.multiple_of(n * 256, 256)
        cols = [pl.ds(pl.multiple_of(s * 128, 128), 128) for s in slots]
        rhs = jnp.concatenate([normal[pl.ds(at, 256), col] for col in cols], axis=1)
        for m in range(2):
            rows = pl.ds(m * 768, 768)
            lhs = jnp.concatenate([wt[s, rows, :] for s in slots], axis=1)
            out = mm(lhs, rhs, 1, 1)
            if last:
                projected[rows, pl.ds(at, 256)] = (total[rows, pl.ds(at, 256)] + out).astype(BF)
            else:
                total[rows, pl.ds(at, 256)] = out


def halves_mask():
    return lax.broadcasted_iota(jnp.int32, (1, 512), 1) % 128 < 64


def side_by_side(block):
    return jnp.concatenate([block[r * 64 : (r + 1) * 64] for r in range(4)], axis=1)


def own_blocks(full, first):
    return jnp.where(first, full[:64], full[64:])


def both_blocks(part, first):
    zero = jnp.zeros_like(part)
    return jnp.concatenate([jnp.where(first, part, zero), jnp.where(first, zero, part)], axis=0)


def places(i):
    g, pair = i // 8, i % 8
    lanes = pl.ds(pl.multiple_of(pair * 128, 128), 128)
    q_rows = pl.ds(pl.multiple_of(g * 256, 256), 256)
    k_rows = pl.ds(pl.multiple_of(QW + g * 64, 64), 64)
    v_rows = pl.ds(pl.multiple_of(QW + KVW + g * 64, 64), 64)
    return g, lanes, q_rows, k_rows, v_rows


def segments():
    row = lax.broadcasted_iota(jnp.int32, (PASS, ROWS), 0)
    lane = lax.broadcasted_iota(jnp.int32, (PASS, ROWS), 1)
    return (lane // TOKENS == row).astype(F32).astype(BF)


UNROLL = 4


def attend(projected, probs, attended, begin, end):
    @pl.loop(begin // UNROLL, end // UNROLL)
    def _(t):
        first = halves_mask()
        ids = [t * UNROLL + u for u in range(UNROLL)]
        spots = [places(i) for i in ids]
        queries = [side_by_side(projected[s[2], s[1]]) for s in spots]
        keys = [projected[s[3], s[1]] for s in spots]
        values = [projected[s[4], s[1]] for s in spots]
        parts = []
        for full in [mm(k, q, 0, 0) for k, q in zip(keys, queries)]:
            scores = own_blocks(full, first) * 0.125
            expo = jnp.exp(scores - jnp.max(scores, axis=0, keepdims=True))
            parts.append((expo * (1.0 / jnp.sum(expo, axis=0, keepdims=True))).astype(BF))
        outs = [mm(v, both_blocks(part, first), 1, 0).astype(BF) for v, part in zip(values, parts)]
        for i, spot, part, out in zip(ids, spots, parts, outs):
            probs[i] = part
            for r in range(4):
                rows = pl.ds(pl.multiple_of(spot[0] * 256 + r * 64, 64), 64)
                attended[rows, spot[1]] = out[:, r * 128 : (r + 1) * 128]


def attend_back(projected, probs, d_att, d_projected, begin, end):
    @pl.loop(begin // UNROLL, end // UNROLL)
    def _(t):
        first = halves_mask()
        ids = [t * UNROLL + u for u in range(UNROLL)]
        spots = [places(i) for i in ids]
        queries = [side_by_side(projected[s[2], s[1]]) for s in spots]
        outs = [side_by_side(d_att[s[2], s[1]]) for s in spots]
        keys = [projected[s[3], s[1]] for s in spots]
        values = [projected[s[4], s[1]] for s in spots]
        parts = [probs[i] for i in ids]
        d_full = [mm(v, da, 0, 0) for v, da in zip(values, outs)]
        dv = [mm(da, both_blocks(part, first), 1, 1).astype(BF) for da, part in zip(outs, parts)]
        d_scores = []
        for full, part in zip(d_full, parts):
            d_probs, wide = own_blocks(full, first), part.astype(F32)
            inner = jnp.sum(wide * d_probs, axis=0, keepdims=True)
            d_scores.append(both_blocks((wide * (d_probs - inner) * 0.125).astype(BF), first))
        dq = [mm(k, ds, 1, 0).astype(BF) for k, ds in zip(keys, d_scores)]
        dk = [mm(q, ds, 1, 1).astype(BF) for q, ds in zip(queries, d_scores)]
        for u, spot in enumerate(spots):
            for r in range(4):
                rows = pl.ds(pl.multiple_of(spot[0] * 256 + r * 64, 64), 64)
                d_projected[rows, spot[1]] = dq[u][:, r * 128 : (r + 1) * 128]
            d_projected[spot[3], spot[1]] = dk[u]
            d_projected[spot[4], spot[1]] = dv[u]


def send(src, dst, sems, slot, where):
    copy = pltpu.make_async_remote_copy(
        src_ref=src,
        dst_ref=dst,
        send_sem=sems[0].at[slot],
        recv_sem=sems[1].at[slot],
        device_id=where,
        device_id_type=pl.DeviceIdType.MESH,
    )
    copy.start()
    return copy


def place():
    return tuple(lax.axis_index(a) for a in ALL)


def greet(peers):
    barrier = pltpu.get_barrier_semaphore()
    for where in peers:
        pl.semaphore_signal(barrier, inc=1, device_id=where, device_id_type=pl.DeviceIdType.MESH)
    pl.semaphore_wait(barrier, len(peers))


def axis_peers(name, at):
    return [{name: (at + j) % 4} for j in (1, 2, 3)]


class Exchange:
    def __init__(self, table, sems):
        z, c, x, y = place()
        group = z * 2 + c
        mine = (group * 4 + x) * 4 + y
        self.table, self.sems, self.used, self.copies = table, sems, 0, []
        self.stages = [
            (axis_peers("y", y), mine, 1),
            (axis_peers("x", x), mine - y, 4),
            ([{"c": 1 - c}], group * 16, 16),
            (axis_peers("z", z), z * 32, 32),
        ]

    def start(self, stage):
        peers, start, size = self.stages[stage]
        block = self.table.at[pl.ds(start, size)]
        self.copies = [send(block, block, self.sems, self.used + j, w) for j, w in enumerate(peers)]
        self.used += len(peers)

    def wait(self):
        for copy in self.copies:
            copy.wait()


def listwise(table, lengths, group):
    length_row = lengths[...].astype(F32)
    row = lax.broadcasted_iota(jnp.int32, (64, 64), 0)
    lane = lax.broadcasted_iota(jnp.int32, (64, 64), 1)
    ends = jnp.sum(jnp.where(lane <= row, length_row, 0.0), axis=1, keepdims=True)
    starts = jnp.sum(jnp.where(lane < row, length_row, 0.0), axis=1, keepdims=True)
    lanes = lax.broadcasted_iota(jnp.int32, (1, 128), 1).astype(F32)
    score, weight, member = [], [], []
    top = jnp.full((64, 128), -1e30, F32)
    labels = jnp.zeros((64, 128), F32)
    for r in range(16):
        both = table[8 * r]
        for j in range(1, 8):
            both = both + table[8 * r + j]
        score.append(both[:, :128])
        weight.append(both[:, 128:])
        position = lanes + 128.0 * r
        member.append(jnp.logical_and(position >= starts, position < ends))
        top = jnp.maximum(top, jnp.where(member[r], score[r], -1e30))
        labels = labels + jnp.where(member[r], weight[r], 0.0)
    peak = jnp.max(top, axis=1, keepdims=True)
    label_total = jnp.sum(labels, axis=1, keepdims=True)
    total = jnp.zeros((64, 128), F32)
    for r in range(16):
        total = total + jnp.exp(jnp.where(member[r], score[r] - peak, -1e30))
    log_norm = peak + jnp.log(jnp.sum(total, axis=1, keepdims=True))
    terms = jnp.zeros((1, 128), F32)
    own = [jnp.zeros((1, 128), F32)] * 2
    for r in range(16):
        norm = jnp.sum(jnp.where(member[r], log_norm, 0.0), axis=0, keepdims=True)
        labels = jnp.sum(jnp.where(member[r], label_total, 0.0), axis=0, keepdims=True)
        log_prob = score[r] - norm
        target = weight[r] / labels
        terms = terms + target * log_prob
        d_score = SCALE * (jnp.exp(log_prob) - target)
        own[r % 2] = own[r % 2] + jnp.where(group == r // 2, d_score, 0.0)
    return -SCALE * jnp.sum(terms, axis=1, keepdims=True), own


ORDER = (2, 1, -1, 0)


class Scatter:
    def __init__(self, blocks, slabs, first, second, third, fourth, sems):
        self.blocks, self.slabs, self.sems = blocks, slabs, sems
        self.first, self.second, self.third, self.fourth = first, second, third, fourth
        self.z, self.c, self.x, self.y = place()
        self.copies = {}

    def at(self, half, stage):
        return self.x if (half + stage) % 2 == 0 else self.y

    def go(self, key, src, dst, half, stage, step):
        name = "xy"[(half + stage) % 2]
        where = {name: (self.at(half, stage) + step) % 4}
        self.copies[key] = send(src, dst, self.sems, len(self.copies), where)

    def part(self, step):
        return pl.ds(0 if step == 1 else 192, 192)

    def wide_first(self, half):
        block = self.blocks.at[half, 2]
        for k, step in enumerate(SIDES):
            self.go((half, 1, step), block.at[:, self.part(step), :], self.first.at[half, k], half, 0, step)

    def rest(self, step):
        return pl.ds(192 if step == 1 else 0, 192)

    def wide_early(self, half, step):
        k, rows = SIDES.index(step), self.rest(step)
        src, dst = self.blocks.at[half, step % 4, :, rows, :], self.second.at[half, k, :, rows, :]
        self.go((half, 2, step), src, dst, half, 0, step)

    def wide_late(self, half, step):
        k, rows, at = SIDES.index(step), self.part(step), step % 4
        self.copies[half, 1, step].wait_recv()
        for b in ORDER:
            slot = (self.at(half, 1) + b) % 4
            mine = self.blocks[half, at, slot, rows, :].astype(F32)
            self.blocks[half, at, slot, rows, :] = (
                mine + self.first[half, k, slot].astype(F32)
            ).astype(BF)
            src, dst = self.blocks.at[half, at, slot, rows, :], self.second.at[half, k, slot, rows, :]
            self.go((half, 2, step, b), src, dst, half, 0, step)

    def wide_last(self):
        for b in ORDER:
            for half in range(2):
                slot = (self.at(half, 1) + b) % 4
                total = self.blocks[half, 0, slot].astype(F32)
                for k, step in enumerate(SIDES):
                    if b == 2:
                        self.copies[half, 2, step].wait_recv()
                    self.copies[half, 2, step, b].wait_recv()
                    total = total + self.second[half, k, slot].astype(F32)
                self.slabs[half, slot] = total.astype(BF)
                slab = self.slabs.at[half, slot]
                if b == 2:
                    for k, step in enumerate(SIDES):
                        src = slab.at[self.part(step), :]
                        self.go((half, 3, step), src, self.third.at[half, k], half, 1, step)
                elif b:
                    k, rows = SIDES.index(b), self.rest(b)
                    dst = self.fourth.at[half, k, rows, :]
                    self.go((half, 4, b), slab.at[rows, :], dst, half, 1, b)

    def narrow_late(self, half):
        for k, step in enumerate(SIDES):
            self.copies[half, 3, step].wait_recv()
            rows = self.part(step)
            at = (self.at(half, 1) + step) % 4
            mine = self.slabs[half, at, rows, :].astype(F32)
            self.slabs[half, at, rows, :] = (mine + self.third[half, k].astype(F32)).astype(BF)
            src, dst = self.slabs.at[half, at, rows, :], self.fourth.at[half, k, rows, :]
            self.go((half, 5, step), src, dst, half, 1, step)

    def narrow_last(self, half):
        total = self.slabs[half, self.at(half, 1)].astype(F32)
        for k, step in enumerate(SIDES):
            self.copies[half, 4, step].wait_recv()
            self.copies[half, 5, step].wait_recv()
            total = total + self.fourth[half, k].astype(F32)
        return total

    def end(self):
        for copy in self.copies.values():
            copy.wait_send()


def outer_peers(z, c):
    return [
        {"z": (z + j) % 4, "c": (c + k) % 2} for j in range(4) for k in range(2) if (j, k) != (0, 0)
    ]


def as_column(row):
    count = row.shape[1]
    same = lax.broadcasted_iota(jnp.int32, (count, count), 0) == lax.broadcasted_iota(
        jnp.int32, (count, count), 1
    )
    return jnp.sum(jnp.where(same, row, 0.0), axis=1, keepdims=True)


def whole_body(
    hidden, gain, w_qkv, w_out_own, final_gain, w_score, prior, labels, lengths,
    loss, grad_qkv, grad_out,
    normal, hsum, wt, total_f, projected, probs, attended, w_blocks, table, pair,
    d_projected, everyone, wide, outer, outer_in,
    leaving, arriving, blocks, slabs, first, second, third, fourth, layers, layers_in,
    qkv_send, qkv_recv, out_send, out_recv, table_send, table_recv,
    pair_send, pair_recv, core_send, core_recv, ring_send, ring_recv, list_send, list_recv,
):
    z, c, x, y = place()
    d_att = attended
    f = x * 4 + y
    group = z * 2 + c

    def qkv_rows(half, part, core):
        start, size = half * 384, 384
        if part is not None:
            start, size = start + part * 192, 192
        return pl.ds(pl.multiple_of(core * 768 + start, 64), size)

    def out_rows(half):
        return pl.ds(pl.multiple_of(c * 32 + half * 16, 16), 16)

    def out_cols(part):
        return pl.ds(0, D) if part is None else pl.ds(part * 1024, 1024)

    def pair_cols(half, part):
        return pl.ds(half * 1536, 1536) if part is None else pl.ds(half * 1536 + part * 768, 768)

    qkv_gather = Gather(
        lambda slot, half, part: wt.at[slot, qkv_rows(half, part, c), :],
        lambda half: wt.at[f, qkv_rows(half, None, c), :],
        (qkv_send, qkv_recv),
        True,
    )
    out_gather = Gather(
        lambda slot, half, part: w_blocks.at[slot, out_rows(half), out_cols(part)],
        lambda half: w_out_own.at[out_rows(half), :],
        (out_send, out_recv),
        True,
    )
    pair_gather = Gather(
        lambda slot, half, part: everyone.at[slot, :, pair_cols(half, part)],
        lambda half: pair.at[:, pair_cols(half, None)],
        (pair_send, pair_recv),
        False,
    )
    scores = Exchange(table, (table_send, table_recv))
    outers = outer_peers(z, c)

    def turned(core):
        for half in range(2):
            cols = pl.ds(pl.multiple_of(core * 768 + half * 384, 128), 384)
            wt[f, qkv_rows(half, None, core), :] = w_qkv[:, cols].T

    turned(c)
    greet(axis_peers("y", y) + axis_peers("x", x) + outers)
    qkv_gather.begin()
    turned(1 - c)
    w_blocks[f] = w_out_own[...]
    norm_rows(hidden, gain, normal, hsum)
    qkv_gather.near_sides()
    qkv_gather.near_opposite()
    out_gather.begin()
    qkv_gather.far_sides()
    out_gather.near_sides()
    qkv_gather.across_sides()
    steps = [(0, 0), (0, 1), (0, -1), (1, 0), (-1, 0), (1, 1), (1, -1), (-1, 1)]
    early = [(x + i) % 4 * 4 + (y + j) % 4 for i, j in steps]
    every = [(i, j) for i in (0, 1, 2, -1) for j in (0, 1, 2, -1)]
    late = [(x + i) % 4 * 4 + (y + j) % 4 for i, j in every if (i, j) not in steps]
    project_part(wt, normal, total_f, projected, early, False, 0, 4)
    qkv_gather.far_opposite()
    out_gather.near_opposite()
    qkv_gather.across_rest()
    project_part(wt, normal, total_f, projected, late, True, 0, 2)
    out_gather.far_sides()
    project_part(wt, normal, total_f, projected, late, True, 2, 4)
    attend(projected, probs, attended, 0, 16)
    out_gather.far_opposite()
    attend(projected, probs, attended, 16, 32)
    out_gather.across_sides()
    out_gather.across_rest()

    w_out = w_blocks[...].reshape(QW, D)
    sums = mm(segments(), attended[...], 1, 1)
    high = sums.astype(BF)
    low = (sums - high.astype(F32)).astype(BF)
    mixed = mm(jnp.concatenate([high, low], axis=0), w_out, 1, 0)
    pooled = (hsum[...] + mixed[:16] + mixed[16:]) * (1.0 / TOKENS)
    inverse = lax.rsqrt(jnp.mean(pooled * pooled, axis=1, keepdims=True) + EPS)
    unit = pooled * inverse
    weight = final_gain[...] * w_score[...]
    score = jnp.sum(unit * weight, axis=1, keepdims=True) + as_column(prior[...])
    mine = group * 16 + f
    row = lax.broadcasted_iota(jnp.int32, (16, 128), 0)
    lane = lax.broadcasted_iota(jnp.int32, (16, 128), 1)
    here = lane == row + mine % 8 * 16
    label_weight = jnp.exp(as_column(labels[...].astype(F32)))
    score_row = jnp.sum(jnp.where(here, score, 0.0), axis=0, keepdims=True)
    label_row = jnp.sum(jnp.where(here, label_weight, 0.0), axis=0, keepdims=True)
    table[mine] = jnp.concatenate([score_row, label_row], axis=1)
    scores.start(0)
    slope = inverse * (weight - unit * jnp.mean(weight * unit, axis=1, keepdims=True))
    slope = (slope * (1.0 / TOKENS)).astype(BF)
    pair[:, :D] = slope
    pair[:, D:] = high
    pair_gather.begin()
    everyone[f] = pair[...]
    d_attended = mm(w_out, slope, 1, 1).astype(BF)
    d_att[...] = mm(d_attended, segments(), 1, 0).astype(BF)
    scores.wait()
    scores.start(1)
    attend_back(projected, probs, d_att, d_projected, 0, 8)
    scores.wait()
    scores.start(2)
    pair_gather.near_sides()
    attend_back(projected, probs, d_att, d_projected, 8, 12)
    scores.wait()
    scores.start(3)
    attend_back(projected, probs, d_att, d_projected, 12, 20)
    pair_gather.near_opposite()
    attend_back(projected, probs, d_att, d_projected, 20, 32)
    scores.wait()
    loss_value, factors = listwise(table, lengths, group)
    loss[...] = loss_value
    own = jnp.where(f // 8 == 0, factors[0], factors[1])
    factor = jnp.sum(jnp.where(here, own, 0.0), axis=1, keepdims=True)
    token = lax.broadcasted_iota(jnp.int32, (PASS, ROWS), 1) // TOKENS
    passage = lax.broadcasted_iota(jnp.int32, (PASS, ROWS), 0)
    factor_row = jnp.sum(jnp.where(token == passage, factor, 0.0), axis=0, keepdims=True)

    @pl.loop(0, 12)
    def _(i):
        at = pl.ds(pl.multiple_of(i * 128, 128), 128)
        d_projected[at, :] = (d_projected[at, :].astype(F32) * factor_row).astype(BF)

    ring = Scatter(blocks, slabs, first, second, third, fourth, (ring_send, ring_recv))
    units = [(step, half) for step in ORDER for half in range(2)]
    swaps = {}

    def unit(step, half):
        if half == 0:
            start = pl.multiple_of((x + step) % 4 * 512, 512)
            rhs = normal[:, pl.ds(start, 512)]
        else:
            at = [pl.multiple_of((i * 4 + (y + step) % 4) * 128, 128) for i in range(4)]
            rhs = jnp.concatenate([normal[:, pl.ds(a, 128)] for a in at], axis=1)
        for parity, target in ((1 - c, leaving), (c, blocks)):
            starts = [pl.multiple_of((4 * half + 2 * i + parity) * 192, 64) for i in range(2)]
            lhs = jnp.concatenate([d_projected[pl.ds(s, 192), :] for s in starts], axis=0)
            out = mm(lhs, rhs, 1, 0).astype(BF)
            for j in range(4):
                target[half, step % 4, j] = out[:, j * 128 : (j + 1) * 128]
        swaps[step, half] = send(
            leaving.at[half, step % 4],
            arriving.at[half, step % 4],
            (core_send, core_recv),
            len(swaps),
            {"c": 1 - c},
        )

    def joined(step, half):
        swaps[step, half].wait_recv()
        at = step % 4
        mine = blocks[half, at].astype(F32)
        blocks[half, at] = (mine + arriving[half, at].astype(F32)).astype(BF)

    def passed(step, half):
        joined(step, half)
        if step == 2:
            ring.wide_first(half)
        elif step:
            ring.wide_early(half, step)

    for n, (step, half) in enumerate(units):
        unit(step, half)
        if n:
            passed(*units[n - 1])
        if n == 3:
            pair_gather.far_sides()
    passed(*units[-1])
    for half in range(2):
        for step in SIDES:
            ring.wide_late(half, step)

    pair_gather.far_opposite()
    lanes = pl.ds(pl.multiple_of(D + f // 2 * 128, 128), 128)
    group_factor = jnp.concatenate([as_column(factors[0]), as_column(factors[1])], axis=0)
    sums = (everyone[:, :, lanes].reshape(256, 128).astype(F32) * group_factor).astype(BF)
    wide[...] = mm(sums, everyone[:, :, :D].reshape(256, D), 0, 0)
    mine = wide[pl.ds(pl.multiple_of(f % 2 * 64, 64), 64), :].astype(BF)
    for l in range(8):
        outer[l] = mine[:, l * 256 : (l + 1) * 256]
    out_copies = [
        send(outer.at[w["z"] * 2 + w["c"]], outer_in.at[k], (list_send, list_recv), k, w)
        for k, w in enumerate(outers)
    ]
    ring.wide_last()
    ring.narrow_late(0)
    ring.narrow_late(1)
    total = outer[z * 2 + c].astype(F32)
    for k, copy in enumerate(out_copies):
        copy.wait()
        total = total + outer_in[k].astype(F32)
    grad_out[...] = total
    for half in range(2):
        both = ring.narrow_last(half).astype(BF)
        layers[2 * half] = both[:192]
        layers[2 * half + 1] = both[192:]
    layer_copies = [
        send(layers.at[(z + j) % 4], layers_in.at[j - 1], (list_send, list_recv), 6 + j, {"z": (z + j) % 4})
        for j in (1, 2, 3)
    ]
    total = layers[z].astype(F32)
    for k, copy in enumerate(layer_copies):
        copy.wait()
        total = total + layers_in[k].astype(F32)
    grad_qkv[...] = total
    qkv_gather.end()
    out_gather.end()
    pair_gather.end()
    ring.end()
    for copy in swaps.values():
        copy.wait_send()


def vm():
    return pl.BlockSpec(memory_space=pltpu.VMEM)


def shape(*dims, dtype=BF):
    return jax.ShapeDtypeStruct(dims, dtype)


def semaphores(count):
    return [pltpu.SemaphoreType.DMA((count,))] * 2


def finish_body(loss, grad_qkv, grad_out, loss_to, qkv_to, out_to):
    loss_to[...] = loss[...]
    qkv_to[...] = grad_qkv[...].T
    out_to[...] = grad_out[...]


def local(hidden, norm_gain, w_qkv, w_out, final_gain, w_score, prior, labels, lengths):
    loss, grad_qkv, grad_out = pl.pallas_call(
        whole_body,
        out_shape=(
            shape(1, 1, dtype=F32),
            shape(192, 128, dtype=F32),
            shape(64, 256, dtype=F32),
        ),
        in_specs=[vm()] * 9,
        out_specs=(vm(),) * 3,
        scratch_shapes=[
            pltpu.VMEM((ROWS, D), BF),
            pltpu.VMEM((PASS, D), F32),
            pltpu.VMEM((16, COLS, 128), BF),
            pltpu.VMEM((COLS, ROWS), F32),
            pltpu.VMEM((COLS, ROWS), BF),
            pltpu.VMEM((32, 64, 512), BF),
            pltpu.VMEM((QW, ROWS), BF),
            pltpu.VMEM((16, 64, D), BF),
            pltpu.VMEM((128, 1, 256), F32),
            pltpu.VMEM((PASS, D + QW), BF),
            pltpu.VMEM((COLS, ROWS), BF),
            pltpu.VMEM((16, PASS, D + QW), BF),
            pltpu.VMEM((128, D), F32),
            pltpu.VMEM((8, 64, 256), BF),
            pltpu.VMEM((7, 64, 256), BF),
            pltpu.VMEM((2, 4, 4, 384, 128), BF),
            pltpu.VMEM((2, 4, 4, 384, 128), BF),
            pltpu.VMEM((2, 4, 4, 384, 128), BF),
            pltpu.VMEM((2, 4, 384, 128), BF),
            pltpu.VMEM((2, 2, 4, 192, 128), BF),
            pltpu.VMEM((2, 2, 4, 384, 128), BF),
            pltpu.VMEM((2, 2, 192, 128), BF),
            pltpu.VMEM((2, 2, 384, 128), BF),
            pltpu.VMEM((4, 192, 128), BF),
            pltpu.VMEM((3, 192, 128), BF),
        ]
        + semaphores(70)
        + semaphores(70)
        + semaphores(10)
        + semaphores(40)
        + semaphores(8)
        + semaphores(36)
        + semaphores(10),
        compiler_params=pltpu.CompilerParams(
            vmem_limit_bytes=VMEM_CAP, has_side_effects=True, collective_id=0
        ),
        name="whole",
    )(
        hidden.reshape(ROWS, D), norm_gain.reshape(1, D), w_qkv, w_out,
        final_gain.reshape(1, D), w_score.reshape(1, D),
        prior.reshape(1, PASS), labels.reshape(1, PASS), lengths.reshape(1, -1),
    )
    loss, grad_qkv, grad_out = pl.pallas_call(
        finish_body,
        out_shape=(
            shape(1, 1, dtype=F32),
            shape(128, 192, dtype=F32),
            shape(64, 256, dtype=F32),
        ),
        in_specs=[vm()] * 3,
        out_specs=(vm(),) * 3,
        compiler_params=pltpu.CompilerParams(vmem_limit_bytes=4 * 1024 * 1024),
        name="finish",
    )(loss, grad_qkv, grad_out)
    return loss.reshape(()), grad_qkv, grad_out


def solution(mesh):
    torus = Mesh(mesh.devices.reshape(4, 2, 4, 4), ALL)
    in_specs = (
        P(ALL, None, None), P(), P(FSDP, None), P(FSDP, None), P(), P(), P(ALL), P(ALL), P(),
    )
    out_specs = (P(), P(FSDP, LIST), P(FSDP, LIST))
    return jax.shard_map(local, mesh=torus, in_specs=in_specs, out_specs=out_specs, check_vma=False)
```

```python
import jax
import jax.numpy as jnp
from jax import lax
from jax.experimental import pallas as pl
from jax.experimental.pallas import tpu as pltpu
from jax.sharding import Mesh
from jax.sharding import PartitionSpec as P

BF = jnp.bfloat16
F32 = jnp.float32
FSDP = ("x", "y")
LIST = ("z", "c")
ALL = ("z", "c", "x", "y")
EPS = 1e-05
SCALE = 64.0
TOKENS = 64
PASS = 16
ROWS = PASS * TOKENS
D = 2048
COLS = 1536
QW = 1024
KVW = 256
VMEM_CAP = 63 * 1024 * 1024


def mm(a, b, ca, cb):
    return lax.dot_general(a, b, (((ca,), (cb,)), ((), ())), preferred_element_type=F32)


def norm_rows(hidden, gain, normal, hsum):
    g = gain[...]

    @pl.loop(0, PASS)
    def _(p):
        at = pl.ds(pl.multiple_of(p * TOKENS, TOKENS), TOKENS)
        x = hidden[at, :].astype(F32)
        mean_square = jnp.mean(x * x, axis=1, keepdims=True)
        normal[at, :] = (x * lax.rsqrt(mean_square + EPS) * g).astype(BF)
        hsum[pl.ds(p, 1), :] = jnp.sum(x, axis=0, keepdims=True)


SIDES = (1, -1)


class Gather:
    def __init__(self, view, own, sems, across):
        self.view, self.own, self.sems, self.across = view, own, sems, across
        self.z, self.c, self.x, self.y = place()
        self.copies = {}

    def slot(self, half, near, far):
        dx, dy = (far, near) if half == 0 else (near, far)
        return (self.x + dx) % 4 * 4 + (self.y + dy) % 4

    def peer(self, half, stage, step):
        name = "yx"[(half + stage) % 2]
        return {name: ((self.y if name == "y" else self.x) + step) % 4}

    def go(self, key, src, dst, where):
        self.copies[key] = send(src, dst, self.sems, len(self.copies), where)

    def pass_on(self, half, near, far):
        slot = self.slot(half, near, far)
        if far == 0:
            for step in SIDES:
                ref = self.view(slot, half, None)
                self.go((half, 2, near, step), ref, ref, self.peer(half, 1, step))
        if self.across:
            ref = self.view(slot, half, None)
            self.go((half, 5, near, far), ref, ref, {"c": 1 - self.c})

    def relay(self, key, half, stage, slot, step):
        ref = self.view(slot, half, 0 if step == 1 else 1)
        self.go(key, ref, ref, self.peer(half, stage, step))

    def begin(self):
        for half in range(2):
            for stage, key in ((0, (half, 1)), (1, (half, 2, 0))):
                for step in SIDES:
                    self.go(
                        (*key, step),
                        self.own(half),
                        self.view(self.slot(half, 0, 0), half, None),
                        self.peer(half, stage, step),
                    )

    def near_sides(self):
        for half in range(2):
            for step in SIDES:
                self.copies[half, 1, step].wait_recv()
                self.relay((half, 3, step), half, 0, self.slot(half, -step, 0), step)
                self.pass_on(half, -step, 0)

    def near_opposite(self):
        for half in range(2):
            for step in SIDES:
                self.copies[half, 3, step].wait_recv()
            self.pass_on(half, 2, 0)

    def far_sides(self):
        for near in (0, 1, -1, 2):
            for half in range(2):
                for step in SIDES:
                    self.copies[half, 2, near, step].wait_recv()
                    slot = self.slot(half, near, -step)
                    self.relay((half, 4, near, step), half, 1, slot, step)
                    self.pass_on(half, near, -step)

    def far_opposite(self, nears=(0, 1, -1, 2)):
        for near in nears:
            for half in range(2):
                for step in SIDES:
                    self.copies[half, 4, near, step].wait_recv()
                self.pass_on(half, near, 2)

    def across_sides(self):
        self.across_wait(lambda near, far: near != 2 and far != 2)

    def across_rest(self):
        self.across_wait(lambda near, far: near == 2 or far == 2)

    def across_wait(self, chosen):
        for key, copy in self.copies.items():
            if key[1] == 5 and chosen(key[2], key[3]):
                copy.wait_recv()

    def end(self):
        for copy in self.copies.values():
            copy.wait_send()


def plane_peers(x, y, c):
    return [{"x": (x + 1) % 4}, {"x": (x + 3) % 4}, {"y": (y + 1) % 4}, {"y": (y + 3) % 4}, {"c": 1 - c}]


def project_part(wt, normal, total, projected, slots, last, begin, end):
    @pl.loop(begin, end)
    def _(n):
        at = pl.multiple_of(n * 256, 256)
        cols = [pl.ds(pl.multiple_of(s * 128, 128), 128) for s in slots]
        rhs = jnp.concatenate([normal[pl.ds(at, 256), col] for col in cols], axis=1)
        for m in range(2):
            rows = pl.ds(m * 768, 768)
            lhs = jnp.concatenate([wt[s, rows, :] for s in slots], axis=1)
            out = mm(lhs, rhs, 1, 1)
            if last:
                projected[rows, pl.ds(at, 256)] = (total[rows, pl.ds(at, 256)] + out).astype(BF)
            else:
                total[rows, pl.ds(at, 256)] = out


def halves_mask():
    return lax.broadcasted_iota(jnp.int32, (1, 512), 1) % 128 < 64


def side_by_side(block):
    return jnp.concatenate([block[r * 64 : (r + 1) * 64] for r in range(4)], axis=1)


def own_blocks(full, first):
    return jnp.where(first, full[:64], full[64:])


def both_blocks(part, first):
    zero = jnp.zeros_like(part)
    return jnp.concatenate([jnp.where(first, part, zero), jnp.where(first, zero, part)], axis=0)


def places(i):
    g, pair = i // 8, i % 8
    lanes = pl.ds(pl.multiple_of(pair * 128, 128), 128)
    q_rows = pl.ds(pl.multiple_of(g * 256, 256), 256)
    k_rows = pl.ds(pl.multiple_of(QW + g * 64, 64), 64)
    v_rows = pl.ds(pl.multiple_of(QW + KVW + g * 64, 64), 64)
    return g, lanes, q_rows, k_rows, v_rows


def segments():
    row = lax.broadcasted_iota(jnp.int32, (PASS, ROWS), 0)
    lane = lax.broadcasted_iota(jnp.int32, (PASS, ROWS), 1)
    return (lane // TOKENS == row).astype(F32).astype(BF)


UNROLL = 4


def attend(projected, probs, attended, begin, end):
    @pl.loop(begin // UNROLL, end // UNROLL)
    def _(t):
        first = halves_mask()
        ids = [t * UNROLL + u for u in range(UNROLL)]
        spots = [places(i) for i in ids]
        queries = [side_by_side(projected[s[2], s[1]]) for s in spots]
        keys = [projected[s[3], s[1]] for s in spots]
        values = [projected[s[4], s[1]] for s in spots]
        parts = []
        for full in [mm(k, q, 0, 0) for k, q in zip(keys, queries)]:
            scores = own_blocks(full, first) * 0.125
            expo = jnp.exp(scores - jnp.max(scores, axis=0, keepdims=True))
            parts.append((expo * (1.0 / jnp.sum(expo, axis=0, keepdims=True))).astype(BF))
        outs = [mm(v, both_blocks(part, first), 1, 0).astype(BF) for v, part in zip(values, parts)]
        for i, spot, part, out in zip(ids, spots, parts, outs):
            probs[i] = part
            for r in range(4):
                rows = pl.ds(pl.multiple_of(spot[0] * 256 + r * 64, 64), 64)
                attended[rows, spot[1]] = out[:, r * 128 : (r + 1) * 128]


def attend_back(projected, probs, d_att, d_projected, begin, end):
    @pl.loop(begin // UNROLL, end // UNROLL)
    def _(t):
        first = halves_mask()
        ids = [t * UNROLL + u for u in range(UNROLL)]
        spots = [places(i) for i in ids]
        queries = [side_by_side(projected[s[2], s[1]]) for s in spots]
        outs = [side_by_side(d_att[s[2], s[1]]) for s in spots]
        keys = [projected[s[3], s[1]] for s in spots]
        values = [projected[s[4], s[1]] for s in spots]
        parts = [probs[i] for i in ids]
        d_full = [mm(v, da, 0, 0) for v, da in zip(values, outs)]
        dv = [mm(da, both_blocks(part, first), 1, 1).astype(BF) for da, part in zip(outs, parts)]
        d_scores = []
        for full, part in zip(d_full, parts):
            d_probs, wide = own_blocks(full, first), part.astype(F32)
            inner = jnp.sum(wide * d_probs, axis=0, keepdims=True)
            d_scores.append(both_blocks((wide * (d_probs - inner) * 0.125).astype(BF), first))
        dq = [mm(k, ds, 1, 0).astype(BF) for k, ds in zip(keys, d_scores)]
        dk = [mm(q, ds, 1, 1).astype(BF) for q, ds in zip(queries, d_scores)]
        for u, spot in enumerate(spots):
            for r in range(4):
                rows = pl.ds(pl.multiple_of(spot[0] * 256 + r * 64, 64), 64)
                d_projected[rows, spot[1]] = dq[u][:, r * 128 : (r + 1) * 128]
            d_projected[spot[3], spot[1]] = dk[u]
            d_projected[spot[4], spot[1]] = dv[u]


def send(src, dst, sems, slot, where):
    copy = pltpu.make_async_remote_copy(
        src_ref=src,
        dst_ref=dst,
        send_sem=sems[0].at[slot],
        recv_sem=sems[1].at[slot],
        device_id=where,
        device_id_type=pl.DeviceIdType.MESH,
    )
    copy.start()
    return copy


def place():
    return tuple(lax.axis_index(a) for a in ALL)


def greet(peers):
    barrier = pltpu.get_barrier_semaphore()
    for where in peers:
        pl.semaphore_signal(barrier, inc=1, device_id=where, device_id_type=pl.DeviceIdType.MESH)
    pl.semaphore_wait(barrier, len(peers))


def axis_peers(name, at):
    return [{name: (at + j) % 4} for j in (1, 2, 3)]


class Exchange:
    def __init__(self, table, sems):
        z, c, x, y = place()
        group = z * 2 + c
        mine = (group * 4 + x) * 4 + y
        self.table, self.sems, self.used, self.copies = table, sems, 0, []
        self.stages = [
            (axis_peers("y", y), mine, 1),
            (axis_peers("x", x), mine - y, 4),
            ([{"c": 1 - c}], group * 16, 16),
            (axis_peers("z", z), z * 32, 32),
        ]

    def start(self, stage):
        peers, start, size = self.stages[stage]
        block = self.table.at[pl.ds(start, size)]
        self.copies = [send(block, block, self.sems, self.used + j, w) for j, w in enumerate(peers)]
        self.used += len(peers)

    def wait(self):
        for copy in self.copies:
            copy.wait()


def listwise(table, lengths, group):
    length_row = lengths[...].astype(F32)
    row = lax.broadcasted_iota(jnp.int32, (64, 64), 0)
    lane = lax.broadcasted_iota(jnp.int32, (64, 64), 1)
    ends = jnp.sum(jnp.where(lane <= row, length_row, 0.0), axis=1, keepdims=True)
    starts = jnp.sum(jnp.where(lane < row, length_row, 0.0), axis=1, keepdims=True)
    lanes = lax.broadcasted_iota(jnp.int32, (1, 128), 1).astype(F32)
    score, weight, member = [], [], []
    top = jnp.full((64, 128), -1e30, F32)
    labels = jnp.zeros((64, 128), F32)
    for r in range(16):
        both = table[8 * r]
        for j in range(1, 8):
            both = both + table[8 * r + j]
        score.append(both[:, :128])
        weight.append(both[:, 128:])
        position = lanes + 128.0 * r
        member.append(jnp.logical_and(position >= starts, position < ends))
        top = jnp.maximum(top, jnp.where(member[r], score[r], -1e30))
        labels = labels + jnp.where(member[r], weight[r], 0.0)
    peak = jnp.max(top, axis=1, keepdims=True)
    label_total = jnp.sum(labels, axis=1, keepdims=True)
    total = jnp.zeros((64, 128), F32)
    for r in range(16):
        total = total + jnp.exp(jnp.where(member[r], score[r] - peak, -1e30))
    log_norm = peak + jnp.log(jnp.sum(total, axis=1, keepdims=True))
    terms = jnp.zeros((1, 128), F32)
    own = [jnp.zeros((1, 128), F32)] * 2
    for r in range(16):
        norm = jnp.sum(jnp.where(member[r], log_norm, 0.0), axis=0, keepdims=True)
        labels = jnp.sum(jnp.where(member[r], label_total, 0.0), axis=0, keepdims=True)
        log_prob = score[r] - norm
        target = weight[r] / labels
        terms = terms + target * log_prob
        d_score = SCALE * (jnp.exp(log_prob) - target)
        own[r % 2] = own[r % 2] + jnp.where(group == r // 2, d_score, 0.0)
    return -SCALE * jnp.sum(terms, axis=1, keepdims=True), own


ORDER = (2, 1, -1, 0)


class Scatter:
    def __init__(self, blocks, slabs, first, second, third, fourth, sems):
        self.blocks, self.slabs, self.sems = blocks, slabs, sems
        self.first, self.second, self.third, self.fourth = first, second, third, fourth
        self.z, self.c, self.x, self.y = place()
        self.copies = {}

    def at(self, half, stage):
        return self.x if (half + stage) % 2 == 0 else self.y

    def go(self, key, src, dst, half, stage, step):
        name = "xy"[(half + stage) % 2]
        where = {name: (self.at(half, stage) + step) % 4}
        self.copies[key] = send(src, dst, self.sems, len(self.copies), where)

    def part(self, step):
        return pl.ds(0 if step == 1 else 192, 192)

    def wide_first(self, half):
        block = self.blocks.at[half, 2]
        for k, step in enumerate(SIDES):
            self.go((half, 1, step), block.at[:, self.part(step), :], self.first.at[half, k], half, 0, step)

    def rest(self, step):
        return pl.ds(192 if step == 1 else 0, 192)

    def wide_early(self, half, step):
        k, rows = SIDES.index(step), self.rest(step)
        src, dst = self.blocks.at[half, step % 4, :, rows, :], self.second.at[half, k, :, rows, :]
        self.go((half, 2, step), src, dst, half, 0, step)

    def wide_late(self, half, step):
        k, rows, at = SIDES.index(step), self.part(step), step % 4
        self.copies[half, 1, step].wait_recv()
        for b in ORDER:
            slot = (self.at(half, 1) + b) % 4
            mine = self.blocks[half, at, slot, rows, :].astype(F32)
            self.blocks[half, at, slot, rows, :] = (
                mine + self.first[half, k, slot].astype(F32)
            ).astype(BF)
            src, dst = self.blocks.at[half, at, slot, rows, :], self.second.at[half, k, slot, rows, :]
            self.go((half, 2, step, b), src, dst, half, 0, step)

    def wide_last(self):
        for b in ORDER:
            for half in range(2):
                slot = (self.at(half, 1) + b) % 4
                total = self.blocks[half, 0, slot].astype(F32)
                for k, step in enumerate(SIDES):
                    if b == 2:
                        self.copies[half, 2, step].wait_recv()
                    self.copies[half, 2, step, b].wait_recv()
                    total = total + self.second[half, k, slot].astype(F32)
                self.slabs[half, slot] = total.astype(BF)
                slab = self.slabs.at[half, slot]
                if b == 2:
                    for k, step in enumerate(SIDES):
                        src = slab.at[self.part(step), :]
                        self.go((half, 3, step), src, self.third.at[half, k], half, 1, step)
                elif b:
                    k, rows = SIDES.index(b), self.rest(b)
                    dst = self.fourth.at[half, k, rows, :]
                    self.go((half, 4, b), slab.at[rows, :], dst, half, 1, b)

    def narrow_late(self, half):
        for k, step in enumerate(SIDES):
            self.copies[half, 3, step].wait_recv()
            rows = self.part(step)
            at = (self.at(half, 1) + step) % 4
            mine = self.slabs[half, at, rows, :].astype(F32)
            self.slabs[half, at, rows, :] = (mine + self.third[half, k].astype(F32)).astype(BF)
            src, dst = self.slabs.at[half, at, rows, :], self.fourth.at[half, k, rows, :]
            self.go((half, 5, step), src, dst, half, 1, step)

    def narrow_last(self, half):
        total = self.slabs[half, self.at(half, 1)].astype(F32)
        for k, step in enumerate(SIDES):
            self.copies[half, 4, step].wait_recv()
            self.copies[half, 5, step].wait_recv()
            total = total + self.fourth[half, k].astype(F32)
        return total

    def end(self):
        for copy in self.copies.values():
            copy.wait_send()


def outer_peers(z, c):
    return [
        {"z": (z + j) % 4, "c": (c + k) % 2} for j in range(4) for k in range(2) if (j, k) != (0, 0)
    ]


def as_column(row):
    count = row.shape[1]
    same = lax.broadcasted_iota(jnp.int32, (count, count), 0) == lax.broadcasted_iota(
        jnp.int32, (count, count), 1
    )
    return jnp.sum(jnp.where(same, row, 0.0), axis=1, keepdims=True)


def whole_body(
    hidden_hbm, gain, w_qkv, w_out_own, final_gain, w_score, prior, labels, lengths,
    loss, grad_qkv, grad_out,
    hidden, hidden_sem, normal, hsum, wt, total_f, projected, probs, attended, w_blocks, table, pair,
    d_projected, everyone, wide, outer, outer_in,
    leaving, arriving, blocks, slabs, first, second, third, fourth, layers, layers_in,
    qkv_send, qkv_recv, out_send, out_recv, table_send, table_recv,
    pair_send, pair_recv, core_send, core_recv, ring_send, ring_recv, list_send, list_recv,
):
    z, c, x, y = place()
    d_att = attended
    f = x * 4 + y
    group = z * 2 + c

    def qkv_rows(half, part, core):
        start, size = half * 384, 384
        if part is not None:
            start, size = start + part * 192, 192
        return pl.ds(pl.multiple_of(core * 768 + start, 64), size)

    def out_rows(half):
        return pl.ds(pl.multiple_of(c * 32 + half * 16, 16), 16)

    def out_cols(part):
        return pl.ds(0, D) if part is None else pl.ds(part * 1024, 1024)

    def pair_cols(half, part):
        return pl.ds(half * 1536, 1536) if part is None else pl.ds(half * 1536 + part * 768, 768)

    qkv_gather = Gather(
        lambda slot, half, part: wt.at[slot, qkv_rows(half, part, c), :],
        lambda half: wt.at[f, qkv_rows(half, None, c), :],
        (qkv_send, qkv_recv),
        True,
    )
    out_gather = Gather(
        lambda slot, half, part: w_blocks.at[slot, out_rows(half), out_cols(part)],
        lambda half: w_out_own.at[out_rows(half), :],
        (out_send, out_recv),
        True,
    )
    pair_gather = Gather(
        lambda slot, half, part: everyone.at[slot, :, pair_cols(half, part)],
        lambda half: pair.at[:, pair_cols(half, None)],
        (pair_send, pair_recv),
        False,
    )
    scores = Exchange(table, (table_send, table_recv))
    outers = outer_peers(z, c)

    def turned(core):
        for half in range(2):
            cols = pl.ds(pl.multiple_of(core * 768 + half * 384, 128), 384)
            wt[f, qkv_rows(half, None, core), :] = w_qkv[:, cols].T

    load = pltpu.make_async_copy(hidden_hbm, hidden, hidden_sem)
    load.start()
    turned(c)
    greet(axis_peers("y", y) + axis_peers("x", x) + outers)
    qkv_gather.begin()
    turned(1 - c)
    w_blocks[f] = w_out_own[...]
    load.wait()
    norm_rows(hidden, gain, normal, hsum)
    qkv_gather.near_sides()
    qkv_gather.near_opposite()
    out_gather.begin()
    qkv_gather.far_sides()
    out_gather.near_sides()
    qkv_gather.across_sides()
    steps = [(0, 0), (0, 1), (0, -1), (1, 0), (-1, 0), (1, 1), (1, -1), (-1, 1)]
    early = [(x + i) % 4 * 4 + (y + j) % 4 for i, j in steps]
    every = [(i, j) for i in (0, 1, 2, -1) for j in (0, 1, 2, -1)]
    late = [(x + i) % 4 * 4 + (y + j) % 4 for i, j in every if (i, j) not in steps]
    project_part(wt, normal, total_f, projected, early, False, 0, 4)
    qkv_gather.far_opposite()
    out_gather.near_opposite()
    qkv_gather.across_rest()
    project_part(wt, normal, total_f, projected, late, True, 0, 2)
    out_gather.far_sides()
    project_part(wt, normal, total_f, projected, late, True, 2, 4)
    attend(projected, probs, attended, 0, 16)
    out_gather.far_opposite()
    attend(projected, probs, attended, 16, 32)
    out_gather.across_sides()
    out_gather.across_rest()

    w_out = w_blocks[...].reshape(QW, D)
    sums = mm(segments(), attended[...], 1, 1)
    high = sums.astype(BF)
    low = (sums - high.astype(F32)).astype(BF)
    mixed = mm(jnp.concatenate([high, low], axis=0), w_out, 1, 0)
    pooled = (hsum[...] + mixed[:16] + mixed[16:]) * (1.0 / TOKENS)
    inverse = lax.rsqrt(jnp.mean(pooled * pooled, axis=1, keepdims=True) + EPS)
    unit = pooled * inverse
    weight = final_gain[...] * w_score[...]
    score = jnp.sum(unit * weight, axis=1, keepdims=True) + as_column(prior[...])
    mine = group * 16 + f
    row = lax.broadcasted_iota(jnp.int32, (16, 128), 0)
    lane = lax.broadcasted_iota(jnp.int32, (16, 128), 1)
    here = lane == row + mine % 8 * 16
    label_weight = jnp.exp(as_column(labels[...].astype(F32)))
    score_row = jnp.sum(jnp.where(here, score, 0.0), axis=0, keepdims=True)
    label_row = jnp.sum(jnp.where(here, label_weight, 0.0), axis=0, keepdims=True)
    table[mine] = jnp.concatenate([score_row, label_row], axis=1)
    scores.start(0)
    slope = inverse * (weight - unit * jnp.mean(weight * unit, axis=1, keepdims=True))
    slope = (slope * (1.0 / TOKENS)).astype(BF)
    pair[:, :D] = slope
    pair[:, D:] = high
    pair_gather.begin()
    everyone[f] = pair[...]
    d_attended = mm(w_out, slope, 1, 1).astype(BF)
    d_att[...] = mm(d_attended, segments(), 1, 0).astype(BF)
    scores.wait()
    scores.start(1)
    attend_back(projected, probs, d_att, d_projected, 0, 8)
    scores.wait()
    scores.start(2)
    pair_gather.near_sides()
    attend_back(projected, probs, d_att, d_projected, 8, 12)
    scores.wait()
    scores.start(3)
    attend_back(projected, probs, d_att, d_projected, 12, 20)
    pair_gather.near_opposite()
    attend_back(projected, probs, d_att, d_projected, 20, 32)
    scores.wait()
    loss_value, factors = listwise(table, lengths, group)
    loss[...] = loss_value
    own = jnp.where(f // 8 == 0, factors[0], factors[1])
    factor = jnp.sum(jnp.where(here, own, 0.0), axis=1, keepdims=True)
    token = lax.broadcasted_iota(jnp.int32, (PASS, ROWS), 1) // TOKENS
    passage = lax.broadcasted_iota(jnp.int32, (PASS, ROWS), 0)
    factor_row = jnp.sum(jnp.where(token == passage, factor, 0.0), axis=0, keepdims=True)

    @pl.loop(0, 12)
    def _(i):
        at = pl.ds(pl.multiple_of(i * 128, 128), 128)
        d_projected[at, :] = (d_projected[at, :].astype(F32) * factor_row).astype(BF)

    ring = Scatter(blocks, slabs, first, second, third, fourth, (ring_send, ring_recv))
    units = [(step, half) for step in ORDER for half in range(2)]
    swaps = {}

    def unit(step, half):
        if half == 0:
            start = pl.multiple_of((x + step) % 4 * 512, 512)
            rhs = normal[:, pl.ds(start, 512)]
        else:
            at = [pl.multiple_of((i * 4 + (y + step) % 4) * 128, 128) for i in range(4)]
            rhs = jnp.concatenate([normal[:, pl.ds(a, 128)] for a in at], axis=1)
        for parity, target in ((1 - c, leaving), (c, blocks)):
            starts = [pl.multiple_of((4 * half + 2 * i + parity) * 192, 64) for i in range(2)]
            lhs = jnp.concatenate([d_projected[pl.ds(s, 192), :] for s in starts], axis=0)
            out = mm(lhs, rhs, 1, 0).astype(BF)
            for j in range(4):
                target[half, step % 4, j] = out[:, j * 128 : (j + 1) * 128]
        swaps[step, half] = send(
            leaving.at[half, step % 4],
            arriving.at[half, step % 4],
            (core_send, core_recv),
            len(swaps),
            {"c": 1 - c},
        )

    def joined(step, half):
        swaps[step, half].wait_recv()
        at = step % 4
        mine = blocks[half, at].astype(F32)
        blocks[half, at] = (mine + arriving[half, at].astype(F32)).astype(BF)

    def passed(step, half):
        joined(step, half)
        if step == 2:
            ring.wide_first(half)
        elif step:
            ring.wide_early(half, step)

    for n, (step, half) in enumerate(units):
        unit(step, half)
        if n:
            passed(*units[n - 1])
        if n == 3:
            pair_gather.far_sides()
    passed(*units[-1])
    for half in range(2):
        for step in SIDES:
            ring.wide_late(half, step)

    pair_gather.far_opposite()
    lanes = pl.ds(pl.multiple_of(D + f // 2 * 128, 128), 128)
    group_factor = jnp.concatenate([as_column(factors[0]), as_column(factors[1])], axis=0)
    sums = (everyone[:, :, lanes].reshape(256, 128).astype(F32) * group_factor).astype(BF)
    wide[...] = mm(sums, everyone[:, :, :D].reshape(256, D), 0, 0)
    mine = wide[pl.ds(pl.multiple_of(f % 2 * 64, 64), 64), :].astype(BF)
    for l in range(8):
        outer[l] = mine[:, l * 256 : (l + 1) * 256]
    out_copies = [
        send(outer.at[w["z"] * 2 + w["c"]], outer_in.at[k], (list_send, list_recv), k, w)
        for k, w in enumerate(outers)
    ]
    ring.wide_last()
    ring.narrow_late(0)
    ring.narrow_late(1)
    total = outer[z * 2 + c].astype(F32)
    for k, copy in enumerate(out_copies):
        copy.wait()
        total = total + outer_in[k].astype(F32)
    grad_out[...] = total
    for half in range(2):
        both = ring.narrow_last(half).astype(BF)
        layers[2 * half] = both[:192]
        layers[2 * half + 1] = both[192:]
    layer_copies = [
        send(layers.at[(z + j) % 4], layers_in.at[j - 1], (list_send, list_recv), 6 + j, {"z": (z + j) % 4})
        for j in (1, 2, 3)
    ]
    total = layers[z].astype(F32)
    for k, copy in enumerate(layer_copies):
        copy.wait()
        total = total + layers_in[k].astype(F32)
    grad_qkv[...] = total
    qkv_gather.end()
    out_gather.end()
    pair_gather.end()
    ring.end()
    for copy in swaps.values():
        copy.wait_send()


def vm():
    return pl.BlockSpec(memory_space=pltpu.VMEM)


def shape(*dims, dtype=BF):
    return jax.ShapeDtypeStruct(dims, dtype)


def semaphores(count):
    return [pltpu.SemaphoreType.DMA((count,))] * 2


def finish_body(loss, grad_qkv, grad_out, loss_to, qkv_to, out_to):
    loss_to[...] = loss[...]
    qkv_to[...] = grad_qkv[...].T
    out_to[...] = grad_out[...]


def local(hidden, norm_gain, w_qkv, w_out, final_gain, w_score, prior, labels, lengths):
    loss, grad_qkv, grad_out = pl.pallas_call(
        whole_body,
        out_shape=(
            shape(1, 1, dtype=F32),
            shape(192, 128, dtype=F32),
            shape(64, 256, dtype=F32),
        ),
        in_specs=[pl.BlockSpec(memory_space=pl.ANY)] + [vm()] * 8,
        out_specs=(vm(),) * 3,
        scratch_shapes=[
            pltpu.VMEM((ROWS, D), BF),
            pltpu.SemaphoreType.DMA,
            pltpu.VMEM((ROWS, D), BF),
            pltpu.VMEM((PASS, D), F32),
            pltpu.VMEM((16, COLS, 128), BF),
            pltpu.VMEM((COLS, ROWS), F32),
            pltpu.VMEM((COLS, ROWS), BF),
            pltpu.VMEM((32, 64, 512), BF),
            pltpu.VMEM((QW, ROWS), BF),
            pltpu.VMEM((16, 64, D), BF),
            pltpu.VMEM((128, 1, 256), F32),
            pltpu.VMEM((PASS, D + QW), BF),
            pltpu.VMEM((COLS, ROWS), BF),
            pltpu.VMEM((16, PASS, D + QW), BF),
            pltpu.VMEM((128, D), F32),
            pltpu.VMEM((8, 64, 256), BF),
            pltpu.VMEM((7, 64, 256), BF),
            pltpu.VMEM((2, 4, 4, 384, 128), BF),
            pltpu.VMEM((2, 4, 4, 384, 128), BF),
            pltpu.VMEM((2, 4, 4, 384, 128), BF),
            pltpu.VMEM((2, 4, 384, 128), BF),
            pltpu.VMEM((2, 2, 4, 192, 128), BF),
            pltpu.VMEM((2, 2, 4, 384, 128), BF),
            pltpu.VMEM((2, 2, 192, 128), BF),
            pltpu.VMEM((2, 2, 384, 128), BF),
            pltpu.VMEM((4, 192, 128), BF),
            pltpu.VMEM((3, 192, 128), BF),
        ]
        + semaphores(70)
        + semaphores(70)
        + semaphores(10)
        + semaphores(40)
        + semaphores(8)
        + semaphores(36)
        + semaphores(10),
        compiler_params=pltpu.CompilerParams(
            vmem_limit_bytes=VMEM_CAP, has_side_effects=True, collective_id=0
        ),
        name="whole",
    )(
        hidden.reshape(ROWS, D), norm_gain.reshape(1, D), w_qkv, w_out,
        final_gain.reshape(1, D), w_score.reshape(1, D),
        prior.reshape(1, PASS), labels.reshape(1, PASS), lengths.reshape(1, -1),
    )
    loss, grad_qkv, grad_out = pl.pallas_call(
        finish_body,
        out_shape=(
            shape(1, 1, dtype=F32),
            shape(128, 192, dtype=F32),
            shape(64, 256, dtype=F32),
        ),
        in_specs=[vm()] * 3,
        out_specs=(vm(),) * 3,
        compiler_params=pltpu.CompilerParams(vmem_limit_bytes=4 * 1024 * 1024),
        name="finish",
    )(loss, grad_qkv, grad_out)
    return loss.reshape(()), grad_qkv, grad_out


def solution(mesh):
    torus = Mesh(mesh.devices.reshape(4, 2, 4, 4), ALL)
    in_specs = (
        P(ALL, None, None), P(), P(FSDP, None), P(FSDP, None), P(), P(), P(ALL), P(ALL), P(),
    )
    out_specs = (P(), P(FSDP, LIST), P(FSDP, LIST))
    return jax.shard_map(local, mesh=torus, in_specs=in_specs, out_specs=out_specs, check_vma=False)
```
